32 devices in a mesh: rep: 2 (over y), shard: 16 (over z, x, core).
Axes of the slice: x: 2, y: 2, z: 4, core: 2. Of those that a mesh axis runs over, the one named last changes fastest.
Arguments:
- tokens: bfloat16 [16384, 896], P(('rep', 'shard')), may hold values from -6 to 6
- cotangent: bfloat16 [16384, 896], P(('rep', 'shard')), may hold values from -6 to 6
- place: int32 [16384], replicated, may hold values from 0 to 16383, as said below
- prefix: int32 [4], replicated, may hold values from 409 to 2048
- attn_norm: bfloat16 [896], P('shard'), may hold values from 0.5 to 1.5
- q_weight: bfloat16 [896, 896], P('shard'), may hold values from -0.1875 to 0.1875
- q_bias: bfloat16 [896], P('shard'), may hold values from -3 to 3
- k_weight: bfloat16 [896, 128], P('shard'), may hold values from -0.1875 to 0.1875
- k_bias: bfloat16 [128], P('shard'), may hold values from -3 to 3
- v_weight: bfloat16 [896, 128], P('shard'), may hold values from -0.1875 to 0.1875
- v_bias: bfloat16 [128], P('shard'), may hold values from -3 to 3
- o_weight: bfloat16 [896, 896], P('shard'), may hold values from -1.5 to 1.5
- mlp_norm: bfloat16 [896], P('shard'), may hold values from 0.5 to 1.5
- gate_weight: bfloat16 [896, 4864], P('shard'), may hold values from -0.1875 to 0.1875
- up_projection_weight: bfloat16 [896, 4864], P('shard'), may hold values from -0.1875 to 0.1875
- down_weight: bfloat16 [4864, 896], P('shard'), may hold values from -0.078125 to 0.078125
Outputs:
- output: bfloat16 [16384, 896], P(('rep', 'shard'))
- input_grad: bfloat16 [16384, 896], P(('rep', 'shard'))
- attn_norm_grad: float32 [896], P('shard')
- q_weight_grad: float32 [896, 896], P('shard')
- q_bias_grad: float32 [896], P('shard')
- k_weight_grad: float32 [896, 128], P('shard')
- k_bias_grad: float32 [128], P('shard')
- v_weight_grad: float32 [896, 128], P('shard')
- v_bias_grad: float32 [128], P('shard')
- o_weight_grad: float32 [896, 896], P('shard')
- mlp_norm_grad: float32 [896], P('shard')
- gate_weight_grad: float32 [896, 4864], P('shard')
- up_weight_grad: float32 [896, 4864], P('shard')
- down_weight_grad: float32 [4864, 896], P('shard')
The draws below stay inside these ranges and needn't reach their ends.
Inputs may be any that keep to these rules, and one draw needn't show every extreme that they name: `place`: each value appears once. Rows of one device in one micro-batch are 256 consecutive positions of one sequence in order; the sequences of one micro-batch of one rep group are wholly held by that group's devices in that micro-batch, in blocks of 256 rows placed on its devices in any order.
All inputs are finite; a program needn't handle non-finite values.
Results may differ from the reference program's by a relative error of at most 0.019.
Values may be sent and summed in bfloat16 or wider, within the bound.
No kernel may reach another device: no remote copies, remote signals or barrier semaphores. Data moves between devices by JAX's collectives and lax.ppermute only.
A program may use at most 256 MiB of HBM per device.

```python
import jax
import jax.numpy as jnp
from jax import lax

D = 896
HEADS = 14
KV_HEADS = 2
HEAD_DIM = 64
FF = 4864
TMB = 256
MB = 2
SEQ = 4096
TOKENS = 16384
NSEQS = 4
N_REP = 2
N_SHARD = 16


def draw_place(key, part):
    group_total = N_REP * MB

    def one_group(item_count):
        order = jax.random.permutation(jax.random.fold_in(key, item_count), N_SHARD)
        span_ids = item_count * N_SHARD + order
        return span_ids[:, None] * TMB + jnp.arange(TMB)[None, :]
    table = jax.vmap(one_group)(jnp.arange(group_total))
    table = table.reshape(N_REP, MB, N_SHARD, TMB).transpose(0, 2, 1, 3)
    return table.reshape(N_REP * N_SHARD * MB * TMB).astype(jnp.int32)


def touch_ends(array, key, least, largest):
    shape = array.shape
    index_at = [jax.random.randint(jax.random.fold_in(key, axis), (), 0, shape[axis]) for axis in range(len(shape))]
    array = array.at[tuple(index_at)].set(least)
    longest = shape.index(max(shape))
    index_at[longest] = (index_at[longest] + 1) % shape[longest]
    return array.at[tuple(index_at)].set(largest)


def shard_levels(stream_key, dims, cuts, low, largest):
    factor_of = 1.0
    for dim, blocks in cuts:
        heights = jax.random.uniform(jax.random.fold_in(jax.random.fold_in(stream_key, 6), dim), (blocks,), jnp.float32, low / len(cuts), largest / len(cuts))
        factor_of = factor_of * jnp.repeat(jnp.exp(heights), dims[dim] // blocks).reshape((-1,) + (1,) * (len(dims) - 1 - dim))
    return factor_of


def noise(stream_key, shape, spread, most, shards=(), kind=jnp.bfloat16):
    loudness = shard_levels(stream_key, shape, shards, -0.22, 0.18) if shards else 1.0
    values = jax.random.normal(stream_key, shape, jnp.float32) * spread * loudness
    return jnp.minimum(jnp.maximum(values, -most), most).astype(kind)


def setup_inputs(seed: int = 0) -> dict:
    key_list = jax.random.split(jax.random.key(seed), 17)
    tokens = noise(key_list[0], (TOKENS, D), 1.0, 6.0, ((0, 32),))
    cotangent = noise(key_list[1], (TOKENS, D), 1.0, 6.0, ((0, 32),))
    place = draw_place(jax.random.fold_in(key_list[16], 71), 0)
    prefix = touch_ends(jax.random.randint(key_list[3], (NSEQS,), SEQ // 10, SEQ // 2 + 1), jax.random.fold_in(key_list[3], 1), SEQ // 10, (SEQ // 2 + 1) - 1).astype(jnp.int32)
    attn_norm = jnp.clip(1.0 + 0.1 * jax.random.normal(key_list[4], (D,), jnp.float32), 0.5, 1.5).astype(jnp.bfloat16)
    q_weight = noise(key_list[5], (D, D), D ** -0.5, 0.1875, ((0, 16),))
    q_bias = noise(key_list[6], (D,), 0.5, 3.0, ((0, 16),))
    k_weight = noise(key_list[7], (D, KV_HEADS * HEAD_DIM), D ** -0.5, 0.1875, ((0, 16),))
    k_bias = noise(key_list[8], (KV_HEADS * HEAD_DIM,), 0.5, 3.0, ((0, 16),))
    v_weight = noise(key_list[9], (D, KV_HEADS * HEAD_DIM), D ** -0.5, 0.1875, ((0, 16),))
    v_bias = noise(key_list[10], (KV_HEADS * HEAD_DIM,), 0.5, 3.0, ((0, 16),))
    o_weight = noise(key_list[11], (D, D), (D // 64) ** -0.5, 1.5, ((0, 16),))
    mlp_norm = jnp.clip(1.0 + 0.1 * jax.random.normal(key_list[12], (D,), jnp.float32), 0.5, 1.5).astype(jnp.bfloat16)
    gate_weight = noise(key_list[13], (D, FF), D ** -0.5, 0.1875, ((0, 16),))
    up_projection_weight = noise(key_list[14], (D, FF), D ** -0.5, 0.1875, ((0, 16),))
    down_weight = noise(key_list[15], (FF, D), FF ** -0.5, 0.078125, ((0, 16),))
    return {"tokens": tokens, "cotangent": cotangent, "place": place, "prefix": prefix, "attn_norm": attn_norm, "q_weight": q_weight, "q_bias": q_bias, "k_weight": k_weight, "k_bias": k_bias, "v_weight": v_weight, "v_bias": v_bias, "o_weight": o_weight, "mlp_norm": mlp_norm, "gate_weight": gate_weight, "up_projection_weight": up_projection_weight, "down_weight": down_weight}


@jax.custom_vjp
def low(v):
    return lax.optimization_barrier(v.astype(jnp.bfloat16)).astype(jnp.float32)

@jax.custom_vjp
def low_back(v):
    return v

def low_keep(v):
    return (low(v), None)

def low_pass(kept, grad):
    return (grad,)

def back_keep(v):
    return (v, None)

def back_low(kept, grad):
    return (low(grad),)
low.defvjp(low_keep, low_pass)
low_back.defvjp(back_keep, back_low)
norm_eps = 1e-06
rope_base = 1000000.0
masked_score = -1e+30

def matmul_high(left_side, right_side):
    return jnp.dot(left_side, right_side, precision=lax.Precision.HIGHEST)

def rms_scale(values, norm_gain):
    factor = lax.rsqrt(lax.optimization_barrier(jnp.mean(values * values, axis=-1, keepdims=True)) + norm_eps)
    return values * factor * norm_gain

def rope_tables(positions):
    half_width = HEAD_DIM // 2
    exponent = jnp.arange(half_width).astype(jnp.float32) * (2.0 / HEAD_DIM)
    frequency = rope_base ** (-exponent)
    angles = positions.astype(jnp.float32)[:, None] * frequency[None, :]
    angles = jnp.concatenate([angles, angles], axis=1)
    return (jnp.cos(angles), jnp.sin(angles))

def rotate(values, cosine, sine_table):
    half_width = HEAD_DIM // 2
    first_half = values[..., :half_width]
    second = values[..., half_width:]
    turned = jnp.concatenate([-second, first_half], axis=-1)
    return values * cosine[:, None, :] + turned * sine_table[:, None, :]

def sequence_layer(params, inputs, prefix_limit):
    attn_gain, q_mat, q_add, k_mat, k_add, v_mat, v_add, o_mat, mlp_gain, gate_mat, up_mat, down_projection_matrix = params
    groups = HEADS // KV_HEADS
    score_scale = HEAD_DIM ** (-0.5)
    normed = low(rms_scale(inputs, attn_gain))
    queries = low_back(matmul_high(normed, q_mat) + q_add).reshape(SEQ, HEADS, HEAD_DIM)
    key_rows = low_back(matmul_high(normed, k_mat) + k_add).reshape(SEQ, KV_HEADS, HEAD_DIM)
    values = low(low_back(matmul_high(normed, v_mat) + v_add)).reshape(SEQ, KV_HEADS, HEAD_DIM)
    positions = jnp.arange(SEQ)
    cosine, sine_table = rope_tables(positions)
    rot_queries = low(rotate(queries, cosine, sine_table)).reshape(SEQ, KV_HEADS, groups, HEAD_DIM)
    rot_keys = low(rotate(key_rows, cosine, sine_table))
    block_rows = min(512, SEQ)

    def attend(item_count):
        block_start = item_count * block_rows
        query_block = lax.dynamic_slice_in_dim(rot_queries, block_start, block_rows, 0)
        attention_scores = jnp.einsum('qkgd,nkd->kgqn', query_block, rot_keys, precision=lax.Precision.HIGHEST)
        attention_scores = low_back(attention_scores * score_scale)
        query_pos = block_start + jnp.arange(block_rows)
        allowed = (positions[None, :] <= query_pos[:, None]) | (positions[None, :] < prefix_limit)
        attention_scores = jnp.where(allowed[None, None], attention_scores, masked_score)
        row_top = lax.optimization_barrier(jnp.max(attention_scores, axis=-1, keepdims=True))
        row_total = row_top + jnp.log(lax.optimization_barrier(jnp.sum(jnp.exp(attention_scores - row_top), axis=-1, keepdims=True)))
        weights = low(jnp.exp(attention_scores - row_total))
        mixed_heads = jnp.einsum('kgqn,nkd->qkgd', weights, values, precision=lax.Precision.HIGHEST)
        return mixed_heads.reshape(block_rows, HEADS * HEAD_DIM)
    attended = lax.map(jax.checkpoint(attend), jnp.arange(SEQ // block_rows))
    attended = low(low_back(attended.reshape(SEQ, HEADS * HEAD_DIM)))
    branch = low_back(matmul_high(attended, o_mat))
    middle = inputs + branch
    normed_two = low(rms_scale(middle, mlp_gain))
    gate_pre = low_back(matmul_high(normed_two, gate_mat))
    up_pre = low_back(matmul_high(normed_two, up_mat))
    hidden = low(jax.nn.silu(gate_pre) * up_pre)
    return middle + low_back(matmul_high(hidden, down_projection_matrix))

def reference(tokens, cotangent, place, prefix, attn_norm, q_weight, q_bias, k_weight, k_bias, v_weight, v_bias, o_weight, mlp_norm, gate_weight, up_projection_weight, down_weight):
    params = tuple((member.astype(jnp.float32) for member in (attn_norm, q_weight, q_bias, k_weight, k_bias, v_weight, v_bias, o_weight, mlp_norm, gate_weight, up_projection_weight, down_weight)))
    order_rows = jnp.zeros((TOKENS,), jnp.int32).at[place].set(jnp.arange(TOKENS).astype(jnp.int32))
    layer_call = jax.checkpoint(sequence_layer)

    def forward(weights_all, inputs):
        ordered = inputs[order_rows].reshape(NSEQS, SEQ, D)

        def scan_step(running, member):
            return (running, layer_call(weights_all, member[0], member[1]))
        _, results = lax.scan(scan_step, jnp.float32(0.0), (ordered, prefix))
        return results.reshape(TOKENS, D)[place]
    result, pullback = jax.vjp(forward, params, tokens.astype(jnp.float32))
    weight_grads, input_grad = pullback(cotangent.astype(jnp.float32))
    return (result.astype(jnp.bfloat16), input_grad.astype(jnp.bfloat16), weight_grads[0], weight_grads[1], weight_grads[2], weight_grads[3], weight_grads[4], weight_grads[5], weight_grads[6], weight_grads[7], weight_grads[8], weight_grads[9], weight_grads[10], weight_grads[11])
```

```python
import functools

import jax
import jax.numpy as jnp
from jax import lax
from jax.experimental import pallas as pl
from jax.experimental.pallas import tpu as pltpu
from jax.sharding import Mesh
from jax.sharding import PartitionSpec as P

HEADS = 14
KV_HEADS = 2
HEAD_DIM = 64
GROUPS = HEADS // KV_HEADS
TMB = 256
MB = 2
SEQ_MAX = 4096
QW = GROUPS * HEAD_DIM
DIRECT_MAX = 8

norm_eps = 1e-06
rope_base = 1000000.0
masked_score = -1e30

bf16 = jnp.bfloat16
f32 = jnp.float32
NN = ((1,), (0,))
NT = ((1,), (1,))
TN = ((0,), (0,))


def mm(a, b, dims=NN):
    return lax.dot_general(a, b, (dims, ((), ())), preferred_element_type=f32)


def swap(a, axis):
    return lax.ppermute(a, axis, [(0, 1), (1, 0)])


def block_mask(kpos, qinfo, b, j):
    ks = kpos[j] + lax.broadcasted_iota(jnp.int32, (TMB, TMB), 0)
    qs = qinfo[b, 0] + lax.broadcasted_iota(jnp.int32, (TMB, TMB), 1)
    return (ks <= qs) | (ks < qinfo[b, 1])


def each_block(count, kind, b, process):
    def step(j, carry):
        @pl.when(kind[b, j] == 1)
        def _():
            process(j, False)

        @pl.when(kind[b, j] == 2)
        def _():
            process(j, True)

        return carry

    lax.fori_loop(0, count, step, 0)


def forward_kernel(count, kind, kpos, qinfo, q_ref, kv_ref, o_ref, lse_ref, m_s, l_s, acc):
    b = pl.program_id(0)
    m_s[...] = jnp.full_like(m_s, masked_score)
    l_s[...] = jnp.zeros_like(l_s)
    acc[...] = jnp.zeros_like(acc)

    def process(j, masked):
        k_rows = kv_ref[j, :HEAD_DIM, :].T
        v_cols = kv_ref[j, HEAD_DIM:, :]
        if masked:
            ok = block_mask(kpos, qinfo, b, j)
        for h in range(GROUPS):
            hs = slice(h * HEAD_DIM, (h + 1) * HEAD_DIM)
            s = mm(k_rows, q_ref[hs, :])
            if masked:
                s = jnp.where(ok, s, masked_score)
            old_max = m_s[h : h + 1, :]
            new_max = jnp.maximum(old_max, jnp.max(s, axis=0, keepdims=True))
            p = jnp.exp(s - new_max)
            fade = jnp.exp(old_max - new_max)
            m_s[h : h + 1, :] = new_max
            l_s[h : h + 1, :] = l_s[h : h + 1, :] * fade + jnp.sum(p, axis=0, keepdims=True)
            acc[hs, :] = acc[hs, :] * fade + mm(v_cols, p.astype(bf16))

    each_block(count, kind, b, process)
    for h in range(GROUPS):
        hs = slice(h * HEAD_DIM, (h + 1) * HEAD_DIM)
        o_ref[hs, :] = acc[hs, :] / l_s[h : h + 1, :]
    lse_ref[...] = m_s[...] + jnp.log(l_s[...])


def attention_forward(kind, kpos, qinfo, q_cols, kv):
    count = kv.shape[0]
    grid_spec = pltpu.PrefetchScalarGridSpec(
        num_scalar_prefetch=3,
        grid=(2,),
        in_specs=[
            pl.BlockSpec((QW, TMB), lambda b, *_: (0, b)),
            pl.BlockSpec((count, 2 * HEAD_DIM, TMB), lambda b, *_: (0, 0, 0)),
        ],
        out_specs=[
            pl.BlockSpec((QW, TMB), lambda b, *_: (0, b)),
            pl.BlockSpec((8, TMB), lambda b, *_: (0, b)),
        ],
        scratch_shapes=[
            pltpu.VMEM((8, TMB), f32),
            pltpu.VMEM((8, TMB), f32),
            pltpu.VMEM((QW, TMB), f32),
        ],
    )
    pairs = count * TMB * TMB * GROUPS
    return pl.pallas_call(
        functools.partial(forward_kernel, count),
        grid_spec=grid_spec,
        out_shape=[
            jax.ShapeDtypeStruct((QW, 2 * TMB), f32),
            jax.ShapeDtypeStruct((8, 2 * TMB), f32),
        ],
        cost_estimate=pl.CostEstimate(
            flops=pairs * 16 * HEAD_DIM,
            transcendentals=pairs,
            bytes_accessed=count * TMB * 4 * HEAD_DIM,
        ),
        compiler_params=pltpu.CompilerParams(dimension_semantics=("arbitrary",)),
        name="attention_forward",
    )(kind, kpos, qinfo, q_cols, kv)


def backward_kernel(
    count, kind, kpos, qinfo, q_ref, kv_ref, do_ref, lse_ref, delta_ref, dq_ref, dkv_ref
):
    b = pl.program_id(0)

    @pl.when(b == 0)
    def _():
        dkv_ref[...] = jnp.zeros_like(dkv_ref)

    dq_ref[...] = jnp.zeros_like(dq_ref)

    def process(j, masked):
        k_cols = kv_ref[j, :HEAD_DIM, :]
        k_rows = k_cols.T
        v_rows = kv_ref[j, HEAD_DIM:, :].T
        if masked:
            ok = block_mask(kpos, qinfo, b, j)
        dk = dv = None
        for h in range(GROUPS):
            hs = slice(h * HEAD_DIM, (h + 1) * HEAD_DIM)
            s = mm(k_rows, q_ref[hs, :])
            if masked:
                s = jnp.where(ok, s, masked_score)
            p = jnp.exp(s - lse_ref[h : h + 1, :])
            dp = mm(v_rows, do_ref[hs, :])
            ds = (p * (dp - delta_ref[h : h + 1, :])).astype(bf16)
            dq_ref[hs, :] += mm(k_cols, ds)
            dk_part = mm(q_ref[hs, :], ds, NT)
            dv_part = mm(do_ref[hs, :], p.astype(bf16), NT)
            dk = dk_part if dk is None else dk + dk_part
            dv = dv_part if dv is None else dv + dv_part
        dkv_ref[j, :HEAD_DIM, :] += dk
        dkv_ref[j, HEAD_DIM:, :] += dv

    each_block(count, kind, b, process)


def attention_backward(kind, kpos, qinfo, q_cols, kv, do_cols, lse, delta):
    count = kv.shape[0]
    grid_spec = pltpu.PrefetchScalarGridSpec(
        num_scalar_prefetch=3,
        grid=(2,),
        in_specs=[
            pl.BlockSpec((QW, TMB), lambda b, *_: (0, b)),
            pl.BlockSpec((count, 2 * HEAD_DIM, TMB), lambda b, *_: (0, 0, 0)),
            pl.BlockSpec((QW, TMB), lambda b, *_: (0, b)),
            pl.BlockSpec((8, TMB), lambda b, *_: (0, b)),
            pl.BlockSpec((8, TMB), lambda b, *_: (0, b)),
        ],
        out_specs=[
            pl.BlockSpec((QW, TMB), lambda b, *_: (0, b)),
            pl.BlockSpec((count, 2 * HEAD_DIM, TMB), lambda b, *_: (0, 0, 0)),
        ],
    )
    pairs = count * TMB * TMB * GROUPS
    return pl.pallas_call(
        functools.partial(backward_kernel, count),
        grid_spec=grid_spec,
        out_shape=[
            jax.ShapeDtypeStruct((QW, 2 * TMB), f32),
            jax.ShapeDtypeStruct((count, 2 * HEAD_DIM, TMB), f32),
        ],
        cost_estimate=pl.CostEstimate(
            flops=pairs * 24 * HEAD_DIM,
            transcendentals=pairs,
            bytes_accessed=count * TMB * 12 * HEAD_DIM,
        ),
        compiler_params=pltpu.CompilerParams(dimension_semantics=("arbitrary",)),
        name="attention_backward",
    )(kind, kpos, qinfo, q_cols, kv, do_cols, lse, delta)


def rotate(values, cosine, sine):
    half = HEAD_DIM // 2
    low, high = values[:, :half], values[:, half:]
    return jnp.concatenate([low * cosine - high * sine, high * cosine + low * sine], axis=1)


def unrotate(grads, cosine, sine):
    half = HEAD_DIM // 2
    low, high = grads[:, :half], grads[:, half:]
    return jnp.concatenate([low * cosine + high * sine, high * cosine - low * sine], axis=1)


def ordered(first, own, other, axis):
    return jnp.where(
        first, jnp.concatenate([own, other], axis), jnp.concatenate([other, own], axis)
    )


def on_device(
    tokens,
    cotangent,
    place,
    prefix,
    attn_norm,
    q_weight,
    q_bias,
    k_weight,
    k_bias,
    v_weight,
    v_bias,
    o_weight,
    mlp_norm,
    gate_weight,
    up_projection_weight,
    down_weight,
):
    chips = lax.axis_size("chip")
    chip = lax.axis_index("chip")
    core = lax.axis_index("core")
    rep = lax.axis_index("rep")
    lead_core = core == 0
    lead_rep = rep == 0
    direct = chips <= DIRECT_MAX
    width = q_weight.shape[1]
    rows = q_weight.shape[0]
    seq_length = min(SEQ_MAX, TMB * chips * 2)
    block_count = 2 * chips

    def gather_chips(a):
        if not direct:
            return lax.all_gather(a, "chip", axis=0, tiled=False)
        parts = [a]
        for k in range(1, chips):
            parts.append(lax.ppermute(a, "chip", [(i, (i + k) % chips) for i in range(chips)]))
        return jnp.stack(parts, axis=0)

    def back_to_chips(chunk_of, order_stack):
        if not direct:
            return lax.psum_scatter(
                order_stack().astype(bf16), "chip", scatter_dimension=0, tiled=False
            ).astype(f32)
        total = chunk_of(0).astype(f32)
        for k in range(1, chips):
            sent = lax.ppermute(
                chunk_of(k).astype(bf16), "chip", [(i, (i - k) % chips) for i in range(chips)]
            )
            total = total + sent.astype(f32)
        return total

    def scatter_chips(stacked):
        def chunk_of(k):
            return lax.dynamic_index_in_dim(stacked, (chip - k) % chips, 0, keepdims=False)

        return back_to_chips(chunk_of, lambda: stacked)

    order = (chip - jnp.arange(chips)) % chips if direct else jnp.arange(chips)
    own_slot = 0 if direct else chip

    with jax.named_scope("weights_qkv"):
        row_pad = -(-(rows + 1) // 16) * 16 - rows - 1
        vectors = jnp.concatenate([attn_norm, mlp_norm, q_bias, k_bias, v_bias])
        vec_count = vectors.shape[0]
        vectors = jnp.pad(vectors, (0, QW + 2 * HEAD_DIM - vec_count))[None]

        def head_columns(c):
            part = jnp.concatenate(
                [
                    q_weight[:, c * QW : (c + 1) * QW],
                    k_weight[:, c * HEAD_DIM : (c + 1) * HEAD_DIM],
                    v_weight[:, c * HEAD_DIM : (c + 1) * HEAD_DIM],
                ],
                axis=1,
            )
            return jnp.pad(jnp.concatenate([part, vectors], axis=0), ((0, row_pad), (0, 0)))

        columns = (head_columns(0), head_columns(1))
        own_columns = jnp.where(lead_core, columns[0], columns[1])
        sent_columns = jnp.where(lead_core, columns[1], columns[0])
        chip_rows = ordered(lead_core, own_columns[None], swap(sent_columns, "core")[None], 0)
        qkv_all = lax.all_gather(chip_rows, "chip", axis=0, tiled=False)
        qkv_full = qkv_all[:, :, :rows].reshape(width, QW + 2 * HEAD_DIM)
        vec_all = qkv_all[:, :, rows, :vec_count].reshape(2 * chips, vec_count).astype(f32)
        kv_rows = k_bias.shape[0]
        gain_one = vec_all[:, :rows].reshape(1, width)
        gain_two = vec_all[:, rows : 2 * rows].reshape(1, width)
        q_add = vec_all[:, 2 * rows : 3 * rows].reshape(2, QW)
        k_add = vec_all[:, 3 * rows : 3 * rows + kv_rows].reshape(2, HEAD_DIM)
        v_add = vec_all[:, 3 * rows + kv_rows :].reshape(2, HEAD_DIM)
        biases = jnp.concatenate([q_add, k_add, v_add], axis=1)
        bias_col = jnp.where(lead_core, biases[0], biases[1])[:, None]

    with jax.named_scope("weights_mlp"):
        ff_rows = down_weight.shape[0]
        half_rows = ff_rows // 2
        half_pad = -(-half_rows // 16) * 16
        quarter = chips * half_pad

        def quarter_columns(w, c):
            split = w.reshape(rows, chips, 2, 2, half_rows)[:, :, c]
            part = jnp.where(lead_rep, split[:, :, 0], split[:, :, 1])
            return jnp.pad(part, ((0, 0), (0, 0), (0, half_pad - half_rows))).reshape(rows, quarter)

        def quarter_pair(c):
            return jnp.concatenate(
                [quarter_columns(gate_weight, c), quarter_columns(up_projection_weight, c)], axis=1
            )

        pairs = (quarter_pair(0), quarter_pair(1))
        own_pair = jnp.where(lead_core, pairs[0], pairs[1])
        sent_pair = jnp.where(lead_core, pairs[1], pairs[0])
        pair_rows = ordered(lead_core, own_pair, swap(sent_pair, "core"), 0)
        gate_up = lax.all_gather(pair_rows, "chip", axis=0, tiled=True)
        down_half = jnp.where(lead_rep, down_weight[:half_rows], down_weight[half_rows:])
        down_half = jnp.pad(down_half, ((0, half_pad - half_rows), (0, 0)))
        o_full = lax.all_gather(o_weight, ("chip", "core"), axis=0, tiled=True)
        down = lax.all_gather(down_half, "chip", axis=0, tiled=True)

    with jax.named_scope("visibility"):
        starts = place.reshape(-1, TMB)[:, 0].reshape(2, chips, 2, MB)
        starts = jnp.where(lead_rep, starts[0], starts[1])
        starts = jnp.where(lead_core, starts, starts[:, ::-1])
        key_starts = starts[order]
        own_starts = starts[chip]
        seq_ids = jnp.arange(prefix.shape[0])
        tables = []
        for m in range(MB):
            ks = key_starts[:, :, m].reshape(block_count)
            qs = own_starts[:, m]
            k_seq, k_pos = ks // seq_length, ks % seq_length
            q_seq, q_pos = qs // seq_length, qs % seq_length
            limit = jnp.sum(
                jnp.where(q_seq[:, None] == seq_ids[None], prefix[None], 0), axis=1
            )
            same = k_seq[None] == q_seq[:, None]
            kp, qp, lim = k_pos[None], q_pos[:, None], limit[:, None]
            full = same & ((kp + TMB - 1 <= qp) | (kp + TMB <= lim))
            part = same & ((kp <= qp + TMB - 1) | (kp < lim))
            kind = jnp.where(full, 1, jnp.where(part, 2, 0)).astype(jnp.int32)
            tables.append((kind, k_pos.astype(jnp.int32), jnp.stack([q_pos, limit], 1)))

    exponent = jnp.arange(HEAD_DIM // 2).astype(f32) * (2.0 / HEAD_DIM)
    frequency = (rope_base ** (-exponent))[:, None]

    def group_rows(a):
        both = jnp.concatenate([a, swap(a, "rep")], axis=0)
        return jnp.concatenate([both, swap(both, "core")], axis=0)

    def group_sum(a):
        half = a.shape[0] // 2
        s = a[:half] + swap(a[half:].astype(bf16), "core").astype(f32)
        half = half // 2
        return s[:half] + swap(s[half:].astype(bf16), "rep").astype(f32)

    def core_pair_sum(a):
        half = a.shape[0] // 2
        return a[:half] + swap(a[half:].astype(bf16), "core").astype(f32)

    fwd = []
    for m in range(MB):
        ms = slice(m * TMB, (m + 1) * TMB)
        with jax.named_scope("project"):
            own = tokens[ms]
            x = own.astype(f32)
            pair = jnp.concatenate([own, swap(own, "core")], axis=0)
            pair_f = pair.astype(f32)
            r_pair = lax.rsqrt(jnp.mean(pair_f * pair_f, axis=-1, keepdims=True) + norm_eps)
            normed = (pair_f * r_pair * gain_one).astype(bf16)
            qkv = mm(qkv_full, normed, ((0,), (1,))) + bias_col
            pos = (tables[m][2][:, :1] + jnp.arange(TMB)[None]).reshape(1, 2 * TMB)
            angles = frequency * pos.astype(f32)
            cosine, sine = jnp.cos(angles)[None], jnp.sin(angles)[None]
            q_rot = rotate(qkv[:QW].reshape(GROUPS, HEAD_DIM, 2 * TMB), cosine, sine)
            q_cols = (q_rot.astype(bf16) * HEAD_DIM**-0.5).astype(bf16).reshape(QW, 2 * TMB)
            k_rot = rotate(qkv[None, QW : QW + HEAD_DIM], cosine, sine)[0].astype(bf16)
            v_cols = qkv[QW + HEAD_DIM :].astype(bf16)
            kv_own = jnp.concatenate([k_rot, v_cols], axis=0)
            kv_own = jnp.stack([kv_own[:, :TMB], kv_own[:, TMB:]], axis=0)
        with jax.named_scope("gather_keys"):
            kv = gather_chips(kv_own).reshape(block_count, 2 * HEAD_DIM, TMB)
        with jax.named_scope("gather_cotangent"):
            cot_group = group_rows(cotangent[ms])
        fwd.append((x, r_pair, normed, cosine, sine, q_cols, kv, cot_group))

    outs, mid = [], []
    for m in range(MB):
        x, r_pair, normed, cosine, sine, q_cols, kv, cot_group = fwd[m]
        heads, lse = attention_forward(*tables[m], q_cols, kv)
        with jax.named_scope("attention_out"):
            att = heads.astype(bf16)
            att_cols = ordered(lead_core, att[:, :TMB], swap(att[:, TMB:], "core"), 0)
            middle = x + mm(att_cols, o_full, TN)
            r2 = lax.rsqrt(jnp.mean(middle * middle, axis=-1, keepdims=True) + norm_eps)
            normed_two = (middle * r2 * gain_two).astype(bf16)
            n2_group = group_rows(normed_two)
        with jax.named_scope("feed_forward"):
            gate_up_pre = mm(n2_group, gate_up)
            gate, up = gate_up_pre[:, :quarter], gate_up_pre[:, quarter:]
            sig = jax.nn.sigmoid(gate)
            silu = gate * sig
            hidden = (silu * up).astype(bf16)
            outs.append((middle + group_sum(mm(hidden, down))).astype(bf16))
        with jax.named_scope("feed_forward_grad"):
            dh = mm(cot_group, down, NT)
            dgate = (dh * up * (sig * (1.0 + gate * (1.0 - sig)))).astype(bf16)
            dup = (dh * silu).astype(bf16)
            dgu = jnp.concatenate([dgate, dup], axis=1)
            dn2 = group_sum(mm(dgu, gate_up, NT))
        mid.append((heads, lse, att_cols, middle, r2, n2_group, hidden, dgu, dn2))

    with jax.named_scope("feed_forward_weight_grads"):
        down_grad = sum(mm(mid[m][6], fwd[m][7], TN) for m in range(MB))
        down_share = lax.psum_scatter(
            down_grad.astype(bf16), "chip", scatter_dimension=0, tiled=True
        )
        gate_up_grad = sum(mm(mid[m][5], mid[m][7], TN) for m in range(MB))
        gate_up_share = lax.psum_scatter(
            gate_up_grad.astype(bf16), "chip", scatter_dimension=0, tiled=True
        )

    o_grad = 0.0
    gain_two_grad = 0.0
    back = []
    for m in range(MB):
        heads, lse, att_cols, middle, r2, _, _, _, dn2 = mid[m]
        x, r_pair, normed, cosine, sine, q_cols, kv, _ = fwd[m]
        ms = slice(m * TMB, (m + 1) * TMB)
        with jax.named_scope("attention_out_grad"):
            gain_two_grad = gain_two_grad + jnp.sum(dn2 * (middle * r2), axis=0)
            e = dn2 * gain_two
            dmiddle = (
                cotangent[ms].astype(f32)
                + r2 * e
                - middle * r2**3 * jnp.mean(e * middle, axis=-1, keepdims=True)
            )
            dbranch = dmiddle.astype(bf16)
            o_grad = o_grad + mm(att_cols, dbranch)
            datt = mm(o_full, dbranch, NT).astype(bf16)
            own_datt = jnp.where(lead_core, datt[:QW], datt[QW:])
            sent_datt = jnp.where(lead_core, datt[QW:], datt[:QW])
            do_cols = jnp.concatenate([own_datt, swap(sent_datt, "core")], axis=1)
            delta = jnp.sum(
                (do_cols.astype(f32) * heads).reshape(GROUPS, HEAD_DIM, 2 * TMB), axis=1
            )
            delta = jnp.pad(delta, ((0, 8 - GROUPS), (0, 0)))
        dq, dkv = attention_backward(*tables[m], q_cols, kv, do_cols, lse, delta)
        with jax.named_scope("return_keys"):
            dkv = dkv.reshape(chips, 2, 2 * HEAD_DIM, TMB)
            dkv_own = back_to_chips(lambda k: dkv[k], lambda: dkv)
            dkv_own = jnp.concatenate([dkv_own[0], dkv_own[1]], axis=1)
        with jax.named_scope("unrotate"):
            dq = unrotate(
                dq.reshape(GROUPS, HEAD_DIM, 2 * TMB) * HEAD_DIM**-0.5, cosine, sine
            ).reshape(QW, 2 * TMB)
            dk = unrotate(dkv_own[None, :HEAD_DIM], cosine, sine)[0]
            dq = dq.astype(bf16)
            dkv_low = jnp.concatenate([dk, dkv_own[HEAD_DIM:]], axis=0).astype(bf16)
        back.append((dmiddle, dq, dkv_low))

    with jax.named_scope("o_weight_grad"):
        o_parts = o_grad.reshape(chips, 2, rows, width)
        o_own = jnp.where(lead_core, o_parts[:, 0], o_parts[:, 1])
        o_sent = jnp.where(lead_core, o_parts[:, 1], o_parts[:, 0])
        o_own = o_own + swap(o_sent.astype(bf16), "core").astype(f32)
        o_share = scatter_chips(o_own)

    with jax.named_scope("project_grad"):
        q_grad = sum(mm(fwd[m][2], back[m][1], ((0,), (1,))) for m in range(MB))
        q_share = scatter_chips(q_grad.reshape(chips, 2 * rows, QW))
        kv_grad = sum(mm(fwd[m][2], back[m][2], ((0,), (1,))) for m in range(MB))
        bias_grad = sum(
            jnp.concatenate(
                [
                    jnp.sum(back[m][1].astype(f32), axis=1),
                    jnp.sum(back[m][2].astype(f32), axis=1),
                ]
            )
            for m in range(MB)
        )
        gain_one_grad = 0.0
        grads_in = []
        for m in range(MB):
            x, r_pair, normed = fwd[m][:3]
            dmiddle, dq, dkv_low = back[m]
            dn1 = core_pair_sum(
                mm(dq, qkv_full[:, :QW], ((0,), (1,)))
                + mm(dkv_low, qkv_full[:, QW:], ((0,), (1,)))
            )
            r1 = r_pair[:TMB]
            gain_one_grad = gain_one_grad + jnp.sum(dn1 * (x * r1), axis=0)
            e1 = dn1 * gain_one
            dx = dmiddle + r1 * e1 - x * r1**3 * jnp.mean(e1 * x, axis=-1, keepdims=True)
            grads_in.append(dx.astype(bf16))

    with jax.named_scope("shares"):
        kv_width = 2 * HEAD_DIM
        packed = jnp.concatenate([bias_grad, gain_one_grad, gain_two_grad])
        pack_count = packed.shape[0]
        pack_rows = -(-pack_count // (kv_width * 16)) * 16
        packed = jnp.pad(packed, (0, pack_rows * kv_width - pack_count)).reshape(
            pack_rows, kv_width
        )
        tail = jnp.concatenate(
            [
                kv_grad.reshape(chips, 2 * rows, kv_width),
                jnp.broadcast_to(packed[None], (chips, pack_rows, kv_width)),
            ],
            axis=1,
        )
        tail_share = scatter_chips(tail)

    def rows_of_core(a):
        own = jnp.where(lead_core, a[:rows], a[rows:])
        sent = jnp.where(lead_core, a[rows:], a[:rows])
        return own, swap(sent, "core")

    def rep_sum(a):
        low = a.astype(bf16)
        return low.astype(f32) + swap(low, "rep").astype(f32)

    with jax.named_scope("owners"):
        o_total = rep_sum(o_share)
        q_own, q_other = rows_of_core(q_share.astype(bf16))
        q_total = rep_sum(ordered(lead_core, q_own, q_other, 1))
        kv_own, kv_other = rows_of_core(tail_share[: 2 * rows].astype(bf16))
        kv_total = rep_sum(ordered(lead_core, kv_own[:, None], kv_other[:, None], 1))
        k_total = kv_total[:, :, :HEAD_DIM].reshape(rows, kv_width)
        v_total = kv_total[:, :, HEAD_DIM:].reshape(rows, kv_width)
        vec = tail_share[2 * rows :].reshape(-1)[:pack_count]
        vec_other = swap(vec.astype(bf16)[None], "core").astype(f32)[0]
        col_count = QW + kv_width
        b_own, b_other = vec[:col_count], vec_other[:col_count]
        bias_all = ordered(lead_core, b_own[None], b_other[None], 0)
        q_b = bias_all[:, :QW].reshape(2 * QW)
        k_b = bias_all[:, QW : QW + HEAD_DIM].reshape(2 * HEAD_DIM)
        v_b = bias_all[:, QW + HEAD_DIM :].reshape(2 * HEAD_DIM)
        gains = vec[col_count:] + vec_other[col_count:]
        everything = rep_sum(jnp.concatenate([q_b, k_b, v_b, gains])[None])[0]
        shard = 2 * chip + core
        sizes = (2 * QW, 2 * HEAD_DIM, 2 * HEAD_DIM, width, width)
        vec_outs, offset = [], 0
        for size in sizes:
            each = size // (2 * chips)
            vec_outs.append(lax.dynamic_slice_in_dim(everything, offset + shard * each, each, 0))
            offset += size
        q_b, k_b, v_b, gain_one_out, gain_two_out = vec_outs

        def whole_columns(part):
            own, other = rows_of_core(part)
            two = ordered(lead_core, own[None], other[None], 0)
            four = ordered(lead_rep, two[None], swap(two, "rep")[None], 0)
            four = four.reshape(2, 2, rows, chips, half_pad)[..., :half_rows]
            return four.transpose(2, 3, 1, 0, 4).reshape(rows, 4 * chips * half_rows).astype(f32)

        gate_out = whole_columns(gate_up_share[:, :quarter])
        up_out = whole_columns(gate_up_share[:, quarter:])
        down_mine = down_share[:half_rows]
        down_out = ordered(lead_rep, down_mine, swap(down_mine, "rep"), 0).astype(f32)

    return (
        jnp.concatenate(outs, axis=0),
        jnp.concatenate(grads_in, axis=0),
        gain_one_out,
        q_total,
        q_b,
        k_total,
        k_b,
        v_total,
        v_b,
        o_total,
        gain_two_out,
        gate_out,
        up_out,
        down_out,
    )


def solution(mesh):
    split = Mesh(mesh.devices.reshape(mesh.shape["rep"], -1, 2), ("rep", "chip", "core"))
    shard = ("chip", "core")
    token_spec = P(("rep", "chip", "core"), None)
    row_spec, vec_spec = P(shard, None), P(shard)
    in_specs = (
        token_spec,
        token_spec,
        P(),
        P(),
        vec_spec,
        row_spec,
        vec_spec,
        row_spec,
        vec_spec,
        row_spec,
        vec_spec,
        row_spec,
        vec_spec,
        row_spec,
        row_spec,
        row_spec,
    )
    out_specs = (token_spec, token_spec) + in_specs[4:]
    return jax.shard_map(
        on_device, mesh=split, in_specs=in_specs, out_specs=out_specs, check_vma=False
    )
```

```python
import functools

import jax
import jax.numpy as jnp
from jax import lax
from jax.experimental import pallas as pl
from jax.experimental.pallas import tpu as pltpu
from jax.sharding import Mesh
from jax.sharding import PartitionSpec as P

HEADS = 14
KV_HEADS = 2
HEAD_DIM = 64
GROUPS = HEADS // KV_HEADS
TMB = 256
MB = 2
SEQ_MAX = 4096
QW = GROUPS * HEAD_DIM
DIRECT_MAX = 8

norm_eps = 1e-06
rope_base = 1000000.0
masked_score = -1e30

bf16 = jnp.bfloat16
f32 = jnp.float32
NN = ((1,), (0,))
NT = ((1,), (1,))
TN = ((0,), (0,))


def mm(a, b, dims=NN):
    return lax.dot_general(a, b, (dims, ((), ())), preferred_element_type=f32)


def swap(a, axis):
    return lax.ppermute(a, axis, [(0, 1), (1, 0)])


class Layout:
    def __init__(self, m, chips, seq_length, rotated):
        self.m, self.chips, self.seq_length, self.rotated = m, chips, seq_length, rotated

    def start(self, starts, ids, chip, second):
        core = jnp.where(second, 1 - ids[2], ids[2])
        return starts[((ids[0] * self.chips + chip) * 2 + core) * MB + self.m]

    def query(self, starts, ids, prefix, b):
        at = self.start(starts, ids, ids[1], b == 1)
        seq = at // self.seq_length
        return seq, at - seq * self.seq_length, prefix[seq]

    def key(self, starts, ids, j):
        chip = j // 2
        if self.rotated:
            chip = ids[1] - chip
            chip = jnp.where(chip < 0, chip + self.chips, chip)
        at = self.start(starts, ids, chip, j % 2 == 1)
        seq = at // self.seq_length
        return seq, at - seq * self.seq_length


def each_block(layout, starts, ids, prefix, process):
    q_seq, q_pos, limit = layout.query(starts, ids, prefix, pl.program_id(0))

    def step(j, carry):
        k_seq, k_pos = layout.key(starts, ids, j)
        same = k_seq == q_seq
        full = same & ((k_pos + TMB - 1 <= q_pos) | (k_pos + TMB <= limit))
        some = same & ((k_pos <= q_pos + TMB - 1) | (k_pos < limit))

        @pl.when(full)
        def _():
            process(j, None)

        @pl.when(some & jnp.logical_not(full))
        def _():
            ks = k_pos + lax.broadcasted_iota(jnp.int32, (TMB, TMB), 0)
            qs = q_pos + lax.broadcasted_iota(jnp.int32, (TMB, TMB), 1)
            process(j, (ks <= qs) | (ks < limit))

        return carry

    lax.fori_loop(0, 2 * layout.chips, step, 0)


def forward_kernel(layout, starts, ids, prefix, q_ref, kv_ref, o_ref, lse_ref, m_s, l_s, acc):
    m_s[...] = jnp.full_like(m_s, masked_score)
    l_s[...] = jnp.zeros_like(l_s)
    acc[...] = jnp.zeros_like(acc)

    def process(j, ok):
        k_rows = kv_ref[j, :HEAD_DIM, :].T
        v_cols = kv_ref[j, HEAD_DIM:, :]
        for h in range(GROUPS):
            hs = slice(h * HEAD_DIM, (h + 1) * HEAD_DIM)
            s = mm(k_rows, q_ref[hs, :])
            if ok is not None:
                s = jnp.where(ok, s, masked_score)
            old_max = m_s[h : h + 1, :]
            new_max = jnp.maximum(old_max, jnp.max(s, axis=0, keepdims=True))
            p = jnp.exp(s - new_max)
            fade = jnp.exp(old_max - new_max)
            m_s[h : h + 1, :] = new_max
            l_s[h : h + 1, :] = l_s[h : h + 1, :] * fade + jnp.sum(p, axis=0, keepdims=True)
            acc[hs, :] = acc[hs, :] * fade + mm(v_cols, p.astype(bf16))

    each_block(layout, starts, ids, prefix, process)
    for h in range(GROUPS):
        hs = slice(h * HEAD_DIM, (h + 1) * HEAD_DIM)
        o_ref[hs, :] = acc[hs, :] / l_s[h : h + 1, :]
    lse_ref[...] = m_s[...] + jnp.log(l_s[...])


def attention_forward(layout, starts, ids, prefix, q_cols, kv):
    count = kv.shape[0]
    grid_spec = pltpu.PrefetchScalarGridSpec(
        num_scalar_prefetch=3,
        grid=(2,),
        in_specs=[
            pl.BlockSpec((QW, TMB), lambda b, *_: (0, b)),
            pl.BlockSpec((count, 2 * HEAD_DIM, TMB), lambda b, *_: (0, 0, 0)),
        ],
        out_specs=[
            pl.BlockSpec((QW, TMB), lambda b, *_: (0, b)),
            pl.BlockSpec((8, TMB), lambda b, *_: (0, b)),
        ],
        scratch_shapes=[
            pltpu.VMEM((8, TMB), f32),
            pltpu.VMEM((8, TMB), f32),
            pltpu.VMEM((QW, TMB), f32),
        ],
    )
    pairs = count * TMB * TMB * GROUPS
    return pl.pallas_call(
        functools.partial(forward_kernel, layout),
        grid_spec=grid_spec,
        out_shape=[
            jax.ShapeDtypeStruct((QW, 2 * TMB), f32),
            jax.ShapeDtypeStruct((8, 2 * TMB), f32),
        ],
        cost_estimate=pl.CostEstimate(
            flops=pairs * 16 * HEAD_DIM,
            transcendentals=pairs,
            bytes_accessed=count * TMB * 4 * HEAD_DIM,
        ),
        compiler_params=pltpu.CompilerParams(dimension_semantics=("arbitrary",)),
        name="attention_forward",
    )(starts, ids, prefix, q_cols, kv)


def backward_kernel(
    layout, starts, ids, prefix, q_ref, kv_ref, do_ref, lse_ref, delta_ref, dq_ref, dkv_ref, acc
):
    b = pl.program_id(0)

    @pl.when(b == 0)
    def _():
        acc[...] = jnp.zeros_like(acc)

    dq_ref[...] = jnp.zeros_like(dq_ref)

    def process(j, ok):
        k_cols = kv_ref[j, :HEAD_DIM, :]
        k_rows = k_cols.T
        v_rows = kv_ref[j, HEAD_DIM:, :].T
        dk = dv = None
        for h in range(GROUPS):
            hs = slice(h * HEAD_DIM, (h + 1) * HEAD_DIM)
            s = mm(k_rows, q_ref[hs, :])
            if ok is not None:
                s = jnp.where(ok, s, masked_score)
            p = jnp.exp(s - lse_ref[h : h + 1, :])
            dp = mm(v_rows, do_ref[hs, :])
            ds = (p * (dp - delta_ref[h : h + 1, :])).astype(bf16)
            dq_ref[hs, :] += mm(k_cols, ds)
            dk_part = mm(q_ref[hs, :], ds, NT)
            dv_part = mm(do_ref[hs, :], p.astype(bf16), NT)
            dk = dk_part if dk is None else dk + dk_part
            dv = dv_part if dv is None else dv + dv_part
        acc[j, :HEAD_DIM, :] += dk
        acc[j, HEAD_DIM:, :] += dv

    each_block(layout, starts, ids, prefix, process)

    @pl.when(b == 1)
    def _():
        dkv_ref[...] = acc[...].astype(bf16)


def attention_backward(layout, starts, ids, prefix, q_cols, kv, do_cols, lse, delta):
    count = kv.shape[0]
    grid_spec = pltpu.PrefetchScalarGridSpec(
        num_scalar_prefetch=3,
        grid=(2,),
        in_specs=[
            pl.BlockSpec((QW, TMB), lambda b, *_: (0, b)),
            pl.BlockSpec((count, 2 * HEAD_DIM, TMB), lambda b, *_: (0, 0, 0)),
            pl.BlockSpec((QW, TMB), lambda b, *_: (0, b)),
            pl.BlockSpec((8, TMB), lambda b, *_: (0, b)),
            pl.BlockSpec((8, TMB), lambda b, *_: (0, b)),
        ],
        out_specs=[
            pl.BlockSpec((QW, TMB), lambda b, *_: (0, b)),
            pl.BlockSpec((count, 2 * HEAD_DIM, TMB), lambda b, *_: (0, 0, 0)),
        ],
        scratch_shapes=[pltpu.VMEM((count, 2 * HEAD_DIM, TMB), f32)],
    )
    pairs = count * TMB * TMB * GROUPS
    return pl.pallas_call(
        functools.partial(backward_kernel, layout),
        grid_spec=grid_spec,
        out_shape=[
            jax.ShapeDtypeStruct((QW, 2 * TMB), f32),
            jax.ShapeDtypeStruct((count, 2 * HEAD_DIM, TMB), bf16),
        ],
        cost_estimate=pl.CostEstimate(
            flops=pairs * 24 * HEAD_DIM,
            transcendentals=pairs,
            bytes_accessed=count * TMB * 12 * HEAD_DIM,
        ),
        compiler_params=pltpu.CompilerParams(dimension_semantics=("arbitrary",)),
        name="attention_backward",
    )(starts, ids, prefix, q_cols, kv, do_cols, lse, delta)


def rotate(values, cosine, sine):
    half = HEAD_DIM // 2
    low, high = values[:, :half], values[:, half:]
    return jnp.concatenate([low * cosine - high * sine, high * cosine + low * sine], axis=1)


def unrotate(grads, cosine, sine):
    half = HEAD_DIM // 2
    low, high = grads[:, :half], grads[:, half:]
    return jnp.concatenate([low * cosine + high * sine, high * cosine - low * sine], axis=1)


def ordered(first, own, other, axis):
    return jnp.where(
        first, jnp.concatenate([own, other], axis), jnp.concatenate([other, own], axis)
    )


def on_device(
    tokens,
    cotangent,
    place,
    prefix,
    attn_norm,
    q_weight,
    q_bias,
    k_weight,
    k_bias,
    v_weight,
    v_bias,
    o_weight,
    mlp_norm,
    gate_weight,
    up_projection_weight,
    down_weight,
):
    chips = lax.axis_size("chip")
    chip = lax.axis_index("chip")
    core = lax.axis_index("core")
    rep = lax.axis_index("rep")
    lead_core = core == 0
    lead_rep = rep == 0
    direct = chips <= DIRECT_MAX
    width = q_weight.shape[1]
    rows = q_weight.shape[0]
    seq_length = min(SEQ_MAX, TMB * chips * 2)
    block_count = 2 * chips

    hop = [[(i, (i + k) % chips) for i in range(chips)] for k in range(chips)]
    back_hop = [[(i, (i - k) % chips) for i in range(chips)] for k in range(chips)]

    def gather_chips(a):
        if not direct:
            return lax.all_gather(a, "chip", axis=0, tiled=False)
        parts = [a] + [lax.ppermute(a, "chip", hop[k]) for k in range(1, chips)]
        return jnp.stack(parts, axis=0)

    def sum_from_chips(chunk_of):
        total = chunk_of(0).astype(f32)
        for k in range(1, chips):
            total = total + lax.ppermute(chunk_of(k), "chip", back_hop[k]).astype(f32)
        return total

    def scatter_chips(stacked):
        if not direct:
            return lax.psum_scatter(stacked, "chip", scatter_dimension=0, tiled=False).astype(f32)

        def chunk_of(k):
            return lax.dynamic_index_in_dim(stacked, (chip - k) % chips, 0, keepdims=False)

        return sum_from_chips(chunk_of)


    cols = QW + 2 * HEAD_DIM
    with jax.named_scope("weights_qkv"):
        vectors = (attn_norm, mlp_norm, q_bias, k_bias, v_bias)
        row_pad = -(rows + len(vectors)) % 16
        vectors = [jnp.pad(v, (0, cols - v.shape[0]))[None] for v in vectors]

        def head_columns(c):
            part = jnp.concatenate(
                [
                    q_weight[:, c * QW : (c + 1) * QW],
                    k_weight[:, c * HEAD_DIM : (c + 1) * HEAD_DIM],
                    v_weight[:, c * HEAD_DIM : (c + 1) * HEAD_DIM],
                ],
                axis=1,
            )
            return jnp.concatenate([part, *vectors, jnp.zeros((row_pad, cols), bf16)], axis=0)

        columns = (head_columns(0), head_columns(1))
        own_columns = jnp.where(lead_core, columns[0], columns[1])
        sent_columns = jnp.where(lead_core, columns[1], columns[0])
        chip_rows = ordered(lead_core, own_columns[None], swap(sent_columns, "core")[None], 0)
        qkv_all = lax.all_gather(chip_rows, "chip", axis=0, tiled=False)
        qkv_full = qkv_all[:, :, :rows].reshape(width, cols)
        vec_all = qkv_all[:, :, rows : rows + len(vectors)].astype(f32)
        vec_all = vec_all.reshape(2 * chips, len(vectors), cols)
        kv_rows = k_bias.shape[0]
        gain_one = vec_all[:, 0, :rows].reshape(1, width)
        gain_two = vec_all[:, 1, :rows].reshape(1, width)
        q_add = vec_all[:, 2, :rows].reshape(2, QW)
        k_add = vec_all[:, 3, :kv_rows].reshape(2, HEAD_DIM)
        v_add = vec_all[:, 4, :kv_rows].reshape(2, HEAD_DIM)
        biases = jnp.concatenate([q_add, k_add, v_add], axis=1)
        bias_col = jnp.where(lead_core, biases[0], biases[1])[:, None]

    with jax.named_scope("weights_mlp"):
        after = chip_rows[1, 0, 0] * 0
        gate_weight, up_projection_weight = gate_weight + after, up_projection_weight + after
        ff_rows = down_weight.shape[0]
        half_rows = ff_rows // 2
        half_pad = -(-half_rows // 16) * 16
        quarter = chips * half_pad

        down_half = jnp.where(lead_rep, down_weight[:half_rows], down_weight[half_rows:])
        o_pair = ordered(lead_core, o_weight, swap(o_weight, "core"), 0)
        o_pad = -(-2 * rows // 16) * 16
        down_o = jnp.concatenate(
            [
                jnp.pad(down_half, ((0, half_pad - half_rows), (0, 0))),
                jnp.pad(o_pair, ((0, o_pad - 2 * rows), (0, 0))),
            ],
            axis=0,
        )
        def quarter_columns(w, c):
            split = w.reshape(rows, chips, 2, 2, half_rows)[:, :, c]
            part = jnp.where(lead_rep, split[:, :, 0], split[:, :, 1])
            return jnp.pad(part, ((0, 0), (0, 0), (0, half_pad - half_rows))).reshape(rows, quarter)

        def quarter_pair(c):
            return jnp.concatenate(
                [quarter_columns(gate_weight, c), quarter_columns(up_projection_weight, c)], axis=1
            )

        pairs = (quarter_pair(0), quarter_pair(1))
        own_pair = jnp.where(lead_core, pairs[0], pairs[1])
        sent_pair = jnp.where(lead_core, pairs[1], pairs[0])
        pair_rows = ordered(lead_core, own_pair, swap(sent_pair, "core"), 0)

    with jax.named_scope("visibility"):
        starts = place.reshape(-1, TMB)[:, 0]
        ids = jnp.stack([rep, chip, core]).astype(jnp.int32)
        layouts = [Layout(m, chips, seq_length, direct and m == 0) for m in range(MB)]

    own_rows = MB * TMB

    def group_rows(a):
        both = jnp.concatenate([a, swap(a, "rep")], axis=0)
        return jnp.concatenate([both, swap(both, "core")], axis=0)

    def core_pair_sum(a):
        half = a.shape[0] // 2
        return a[:half] + swap(a[half:].astype(bf16), "core").astype(f32)

    def rep_pair_sum(a):
        half = a.shape[0] // 2
        return a[:half] + swap(a[half:].astype(bf16), "rep").astype(f32)

    def micro(a, m):
        return jnp.concatenate(
            [a[:, m * TMB : (m + 1) * TMB], a[:, own_rows + m * TMB : own_rows + (m + 1) * TMB]],
            axis=1,
        )

    def both_micros(parts):
        return jnp.concatenate([p[:, :TMB] for p in parts] + [p[:, TMB:] for p in parts], axis=1)

    with jax.named_scope("gather_cotangent"):
        cot_rep = swap(cotangent, "rep")
        cot_parts = (cotangent, cot_rep, swap(cotangent, "core"), swap(cot_rep, "core"))
        qkv_full, cot_parts = lax.optimization_barrier((qkv_full, cot_parts))
        cot_group = jnp.concatenate(cot_parts, axis=0)
    with jax.named_scope("project"):
        x = tokens.astype(f32)
        pair = jnp.concatenate([tokens, swap(tokens, "core")], axis=0).astype(f32)
        r_pair = lax.rsqrt(jnp.mean(pair * pair, axis=-1, keepdims=True) + norm_eps)
        normed = (pair * r_pair * gain_one).astype(bf16)
        qkv = mm(qkv_full, normed, ((0,), (1,))) + bias_col
        exponent = jnp.arange(HEAD_DIM // 2).astype(f32) * (2.0 / HEAD_DIM)
        frequency = (rope_base ** (-exponent))[:, None]
        pos = lax.dynamic_slice_in_dim(starts, (rep * chips + chip) * 2 * MB, 2 * MB) % seq_length
        pos = ordered(lead_core, pos[:MB], pos[MB:], 0)
        pos = (pos[:, None] + jnp.arange(TMB)[None]).reshape(1, 2 * own_rows)
        angles = frequency * pos.astype(f32)
        cosine, sine = jnp.cos(angles)[None], jnp.sin(angles)[None]
        k_rot = rotate(qkv[None, QW : QW + HEAD_DIM], cosine, sine)[0].astype(bf16)
        kv_own = jnp.concatenate([k_rot, qkv[QW + HEAD_DIM :].astype(bf16)], axis=0)
        q_rot = rotate(qkv[:QW].reshape(GROUPS, HEAD_DIM, 2 * own_rows), cosine, sine)
        q_all = (q_rot.astype(bf16) * HEAD_DIM**-0.5).astype(bf16).reshape(QW, 2 * own_rows)
        q_cols = [micro(q_all, m) for m in range(MB)]
    kv = []
    with jax.named_scope("gather_keys"):
        for m in range(MB):
            mine = micro(kv_own, m)
            mine = jnp.stack([mine[:, :TMB], mine[:, TMB:]], axis=0)
            every = gather_chips(mine) if m == 0 else lax.all_gather(mine, "chip", axis=0)
            kv.append(every.reshape(block_count, 2 * HEAD_DIM, TMB))
    with jax.named_scope("gather_mlp"):
        kv[0], down_o, pair_rows = lax.optimization_barrier((kv[0], down_o, pair_rows))
        down_o_all = lax.all_gather(down_o, "chip", axis=0, tiled=False)
        down = down_o_all[:, :half_pad].reshape(quarter, width)
        o_full = down_o_all[:, half_pad : half_pad + 2 * rows].reshape(width, width)

        gate_up = lax.all_gather(pair_rows, "chip", axis=0, tiled=True)

    heads, lse = [], []
    for m in range(MB):
        o_m, lse_m = attention_forward(layouts[m], starts, ids, prefix, q_cols[m], kv[m])
        heads.append(o_m)
        lse.append(lse_m)
    with jax.named_scope("attention_out"):
        att = both_micros([h.astype(bf16) for h in heads])
        att_cols = ordered(lead_core, att[:, :own_rows], swap(att[:, own_rows:], "core"), 0)
        middle = x + mm(att_cols, o_full, TN)
        r2 = lax.rsqrt(jnp.mean(middle * middle, axis=-1, keepdims=True) + norm_eps)
        normed_two = (middle * r2 * gain_two).astype(bf16)
        n2_group = group_rows(normed_two)
    with jax.named_scope("feed_forward"):
        gate_up_pre = mm(n2_group, gate_up)
        gate, up = gate_up_pre[:, :quarter], gate_up_pre[:, quarter:]
        sig = jax.nn.sigmoid(gate)
        silu = gate * sig
        hidden = (silu * up).astype(bf16)
    with jax.named_scope("feed_forward_grad"):
        dh = mm(cot_group, down, NT)
        dgate = (dh * up * (sig * (1.0 + gate * (1.0 - sig)))).astype(bf16)
        dup = (dh * silu).astype(bf16)
        dgu = jnp.concatenate([dgate, dup], axis=1)
        dn2 = rep_pair_sum(core_pair_sum(mm(dgu, gate_up, NT)))
    with jax.named_scope("feed_forward_out"):
        result_half = core_pair_sum(mm(hidden, down))

    with jax.named_scope("attention_out_grad"):
        gain_two_grad = jnp.sum(dn2 * (middle * r2), axis=0)
        e = dn2 * gain_two
        dmiddle = (
            cotangent.astype(f32)
            + r2 * e
            - middle * r2**3 * jnp.mean(e * middle, axis=-1, keepdims=True)
        )
        dbranch = dmiddle.astype(bf16)
        datt = mm(o_full, dbranch, NT).astype(bf16)
        own_datt = jnp.where(lead_core, datt[:QW], datt[QW:])
        sent_datt = jnp.where(lead_core, datt[QW:], datt[:QW])
        datt_all = jnp.concatenate([own_datt, swap(sent_datt, "core")], axis=1)
    with jax.named_scope("o_weight_grad"):
        o_parts = mm(att_cols, dbranch).reshape(chips, 2, rows, width)
        o_own = jnp.where(lead_core, o_parts[:, 0], o_parts[:, 1])
        o_sent = jnp.where(lead_core, o_parts[:, 1], o_parts[:, 0])
        o_own = (o_own + swap(o_sent.astype(bf16), "core").astype(f32)).astype(bf16)
    with jax.named_scope("feed_forward_weight_grads"):
        down_grad = mm(hidden, cot_group, TN).astype(bf16).reshape(chips, half_pad, width)
        gate_up_grad = mm(n2_group, dgu, TN).astype(bf16).reshape(chips, 2 * rows, 2 * quarter)
        pieces = []
        for start in range(0, 2 * quarter, width):
            piece = gate_up_grad[:, :, start : start + width]
            pieces.append(jnp.pad(piece, ((0, 0), (0, 0), (0, width - piece.shape[2]))))
        blob_rows = half_pad + 2 * rows * len(pieces) + rows
        blob_pad = jnp.zeros((chips, -blob_rows % 16, width), bf16)
        blob = jnp.concatenate([down_grad] + pieces + [o_own, blob_pad], axis=1)
        blob = blob.reshape(-1, width)
        datt_all, blob = lax.optimization_barrier((datt_all, blob))
        blob_share = lax.psum_scatter(blob, "chip", scatter_dimension=0, tiled=True)
        down_share = blob_share[:half_pad]
        gate_up_share = jnp.concatenate(
            [
                blob_share[half_pad + 2 * rows * i : half_pad + 2 * rows * (i + 1)]
                for i in range(len(pieces))
            ],
            axis=1,
        )[:, : 2 * quarter]
        o_share = blob_share[blob_rows - rows : blob_rows]
    dq, dkv = [], []
    for m in range(MB):
        with jax.named_scope("attention_out_grad"):
            do_cols = micro(datt_all, m)
            delta = jnp.sum(
                (do_cols.astype(f32) * heads[m]).reshape(GROUPS, HEAD_DIM, 2 * TMB), axis=1
            )
            delta = jnp.pad(delta, ((0, 8 - GROUPS), (0, 0)))
        dq_m, dkv_m = attention_backward(
            layouts[m], starts, ids, prefix, q_cols[m], kv[m], do_cols, lse[m], delta
        )
        dq.append(dq_m)
        dkv.append(dkv_m.reshape(chips, 2, 2 * HEAD_DIM, TMB))
    with jax.named_scope("feed_forward_out"):
        dq[0], result_half = lax.optimization_barrier((dq[0], result_half))
        result = (middle + rep_pair_sum(result_half)).astype(bf16)
    with jax.named_scope("return_keys"):
        if direct:


            def returned(k):
                later = lax.dynamic_index_in_dim(dkv[1], (chip - k) % chips, 0, keepdims=False)
                return jnp.stack([dkv[0][k], later], axis=0)

            dkv_sum = sum_from_chips(returned)
        else:
            dkv_sum = lax.psum_scatter(
                jnp.stack(dkv, axis=1), "chip", scatter_dimension=0, tiled=False
            ).astype(f32)
        dkv = [jnp.concatenate([dkv_sum[m, 0], dkv_sum[m, 1]], axis=1) for m in range(MB)]
    with jax.named_scope("unrotate"):
        dq_all = both_micros(dq).reshape(GROUPS, HEAD_DIM, 2 * own_rows) * HEAD_DIM**-0.5
        dq_low = unrotate(dq_all, cosine, sine).reshape(QW, 2 * own_rows).astype(bf16)
        dkv_all = both_micros(dkv)
        dk = unrotate(dkv_all[None, :HEAD_DIM], cosine, sine)[0]
        dkv_low = jnp.concatenate([dk, dkv_all[HEAD_DIM:]], axis=0).astype(bf16)

    with jax.named_scope("project_grad"):
        q_grad = mm(normed, dq_low, ((0,), (1,))).astype(bf16)
        dn1 = core_pair_sum(
            mm(dq_low, qkv_full[:, :QW], ((0,), (1,)))
            + mm(dkv_low, qkv_full[:, QW:], ((0,), (1,)))
        )
        kv_grad = mm(normed, dkv_low, ((0,), (1,))).astype(bf16)
        qkv_grad = jnp.concatenate([q_grad, kv_grad], axis=1)
        bias_grad = [jnp.sum(g.astype(f32), axis=1) for g in (dq_low, dkv_low)]
        r1 = r_pair[:own_rows]
        gain_one_grad = jnp.sum(dn1 * (x * r1), axis=0)
        e1 = dn1 * gain_one
        dx = dmiddle + r1 * e1 - x * r1**3 * jnp.mean(e1 * x, axis=-1, keepdims=True)
        input_grad = dx.astype(bf16)
    with jax.named_scope("shares"):
        packed = jnp.concatenate(bias_grad + [gain_one_grad, gain_two_grad])
        pack_count = packed.shape[0]
        pack_rows = -(-pack_count // (cols * 16)) * 16
        packed = jnp.pad(packed, (0, pack_rows * cols - pack_count)).reshape(pack_rows, cols)
        share = scatter_chips(
            jnp.concatenate(
                [
                    jnp.broadcast_to(packed.astype(bf16)[None], (chips, pack_rows, cols)),
                    qkv_grad.reshape(chips, 2 * rows, cols),
                ],
                axis=1,
            )
        ).astype(bf16)

    def rep_sum(a):
        return a.astype(f32) + swap(a, "rep").astype(f32)

    with jax.named_scope("owners"):
        o_total = rep_sum(o_share)

        def both_cores(head, body):
            own = jnp.where(lead_core, body[:rows], body[rows:])
            sent = jnp.where(lead_core, body[rows:], body[:rows])
            own = jnp.concatenate([head, own], axis=0)
            other = swap(jnp.concatenate([head, sent], axis=0), "core")
            return rep_sum(ordered(lead_core, own[None], other[None], 0))

        both = both_cores(share[:pack_rows], share[pack_rows:])
        w_both = both[:, pack_rows:]
        k_at, v_at = QW, QW + HEAD_DIM
        q_total = jnp.concatenate([w_both[0, :, :k_at], w_both[1, :, :k_at]], axis=1)
        k_total = jnp.concatenate([w_both[0, :, k_at:v_at], w_both[1, :, k_at:v_at]], axis=1)
        v_total = jnp.concatenate([w_both[0, :, v_at:], w_both[1, :, v_at:]], axis=1)
        vec = both[:, :pack_rows].reshape(2, pack_rows * cols)[:, :pack_count]
        gains = vec[0, cols:] + vec[1, cols:]
        everything = jnp.concatenate(
            [
                vec[:, :QW].reshape(2 * QW),
                vec[:, k_at:v_at].reshape(2 * HEAD_DIM),
                vec[:, v_at:cols].reshape(2 * HEAD_DIM),
                gains,
            ]
        )
        shard = 2 * chip + core
        vec_outs, offset = [], 0
        for size in (2 * QW, 2 * HEAD_DIM, 2 * HEAD_DIM, width, width):
            each = size // (2 * chips)
            vec_outs.append(lax.dynamic_slice_in_dim(everything, offset + shard * each, each, 0))
            offset += size
        q_b, k_b, v_b, gain_one_out, gain_two_out = vec_outs

        mine = jnp.where(lead_core, gate_up_share[:rows], gate_up_share[rows:])
        sent = jnp.where(lead_core, gate_up_share[rows:], gate_up_share[:rows])
        two = ordered(lead_core, mine[None], swap(sent, "core")[None], 0)
        four = ordered(lead_rep, two[None], swap(two, "rep")[None], 0)

        def whole_columns(part):
            part = part.reshape(2, 2, rows, chips, half_pad)[..., :half_rows]
            return part.transpose(2, 3, 1, 0, 4).reshape(rows, 4 * chips * half_rows).astype(f32)

        gate_out = whole_columns(four[..., :quarter])
        up_out = whole_columns(four[..., quarter:])
        down_mine = down_share[:half_rows]
        down_out = ordered(lead_rep, down_mine, swap(down_mine, "rep"), 0).astype(f32)

    return (
        result,
        input_grad,
        gain_one_out,
        q_total,
        q_b,
        k_total,
        k_b,
        v_total,
        v_b,
        o_total,
        gain_two_out,
        gate_out,
        up_out,
        down_out,
    )


def solution(mesh):
    split = Mesh(mesh.devices.reshape(mesh.shape["rep"], -1, 2), ("rep", "chip", "core"))
    shard = ("chip", "core")
    token_spec = P(("rep", "chip", "core"), None)
    row_spec, vec_spec = P(shard, None), P(shard)
    in_specs = (
        token_spec,
        token_spec,
        P(),
        P(),
        vec_spec,
        row_spec,
        vec_spec,
        row_spec,
        vec_spec,
        row_spec,
        vec_spec,
        row_spec,
        vec_spec,
        row_spec,
        row_spec,
        row_spec,
    )
    out_specs = (token_spec, token_spec) + in_specs[4:]
    return jax.shard_map(
        on_device, mesh=split, in_specs=in_specs, out_specs=out_specs, check_vma=False
    )
```

```python
import functools

import jax
import jax.numpy as jnp
from jax import lax
from jax.experimental import pallas as pl
from jax.experimental.pallas import tpu as pltpu
from jax.sharding import Mesh
from jax.sharding import PartitionSpec as P

HEADS = 14
KV_HEADS = 2
HEAD_DIM = 64
GROUPS = HEADS // KV_HEADS
TMB = 256
MB = 2
SEQ_MAX = 4096
QW = GROUPS * HEAD_DIM
DIRECT_MAX = 8
FORWARD_AHEAD = 4
BACKWARD_AHEAD = 2

norm_eps = 1e-06
rope_base = 1000000.0
masked_score = -1e30

bf16 = jnp.bfloat16
f32 = jnp.float32
NN = ((1,), (0,))
NT = ((1,), (1,))
TN = ((0,), (0,))


def mm(a, b, dims=NN):
    return lax.dot_general(a, b, (dims, ((), ())), preferred_element_type=f32)


def swap(a, axis):
    return lax.ppermute(a, axis, [(0, 1), (1, 0)])


class Layout:
    def __init__(self, m, chips, seq_length, rotated):
        self.m, self.chips, self.seq_length, self.rotated = m, chips, seq_length, rotated

    def start(self, starts, ids, chip, second):
        core = jnp.where(second, 1 - ids[2], ids[2])
        return starts[((ids[0] * self.chips + chip) * 2 + core) * MB + self.m]

    def query(self, starts, ids, prefix, b):
        at = self.start(starts, ids, ids[1], b == 1)
        seq = at // self.seq_length
        return seq, at - seq * self.seq_length, prefix[seq]

    def key_chip(self, ids, j):
        chip = j // 2
        if self.rotated:
            chip = ids[1] - chip
            chip = jnp.where(chip < 0, chip + self.chips, chip)
        return chip

    def slot(self, ids, j):
        return 2 * self.key_chip(ids, j) + j % 2

    def key(self, starts, ids, j):
        chip = self.key_chip(ids, j)
        at = self.start(starts, ids, chip, j % 2 == 1)
        seq = at // self.seq_length
        return seq, at - seq * self.seq_length


def each_block(layout, starts, ids, prefix, process):
    q_seq, q_pos, limit = layout.query(starts, ids, prefix, pl.program_id(0))

    def step(j, carry):
        k_seq, k_pos = layout.key(starts, ids, j)
        same = k_seq == q_seq
        full = same & ((k_pos + TMB - 1 <= q_pos) | (k_pos + TMB <= limit))
        some = same & ((k_pos <= q_pos + TMB - 1) | (k_pos < limit))

        @pl.when(full)
        def _():
            process(j, None)

        @pl.when(some & jnp.logical_not(full))
        def _():
            ks = k_pos + lax.broadcasted_iota(jnp.int32, (TMB, TMB), 0)
            qs = q_pos + lax.broadcasted_iota(jnp.int32, (TMB, TMB), 1)
            process(j, (ks <= qs) | (ks < limit))

        return carry

    lax.fori_loop(0, 2 * layout.chips, step, 0)


def forward_kernel(layout, starts, ids, prefix, q_ref, kv_ref, o_ref, lse_ref, m_s, l_s, acc):
    m_s[...] = jnp.full_like(m_s, masked_score)
    l_s[...] = jnp.zeros_like(l_s)
    acc[...] = jnp.zeros_like(acc)

    def process(j, ok):
        k_rows = kv_ref[j, :HEAD_DIM, :].T
        v_cols = kv_ref[j, HEAD_DIM:, :]
        old_max, old_sum = m_s[...], l_s[...]
        maxes, sums = [], []

        def score(h):
            s = mm(k_rows, q_ref[h * HEAD_DIM : (h + 1) * HEAD_DIM, :])
            return s if ok is None else jnp.where(ok, s, masked_score)

        ahead = [score(h) for h in range(FORWARD_AHEAD)]
        for h in range(GROUPS):
            if h + FORWARD_AHEAD < GROUPS:
                ahead.append(score(h + FORWARD_AHEAD))
            s = ahead.pop(0)
            hs = slice(h * HEAD_DIM, (h + 1) * HEAD_DIM)
            head_max = old_max[h : h + 1, :]
            new_max = jnp.maximum(head_max, jnp.max(s, axis=0, keepdims=True))
            p = jnp.exp(s - new_max)
            fade = jnp.exp(head_max - new_max)
            maxes.append(new_max)
            sums.append(old_sum[h : h + 1, :] * fade + jnp.sum(p, axis=0, keepdims=True))
            acc[hs, :] = acc[hs, :] * fade + mm(v_cols, p.astype(bf16))
        m_s[...] = jnp.concatenate(maxes + [old_max[GROUPS:]], axis=0)
        l_s[...] = jnp.concatenate(sums + [old_sum[GROUPS:]], axis=0)

    each_block(layout, starts, ids, prefix, process)
    for h in range(GROUPS):
        hs = slice(h * HEAD_DIM, (h + 1) * HEAD_DIM)
        o_ref[hs, :] = acc[hs, :] / l_s[h : h + 1, :]
    lse_ref[...] = m_s[...] + jnp.log(l_s[...])


def attention_forward(layout, starts, ids, prefix, q_cols, kv):
    count = kv.shape[0]
    grid_spec = pltpu.PrefetchScalarGridSpec(
        num_scalar_prefetch=3,
        grid=(2,),
        in_specs=[
            pl.BlockSpec((QW, TMB), lambda b, *_: (0, b)),
            pl.BlockSpec((count, 2 * HEAD_DIM, TMB), lambda b, *_: (0, 0, 0)),
        ],
        out_specs=[
            pl.BlockSpec((QW, TMB), lambda b, *_: (0, b)),
            pl.BlockSpec((8, TMB), lambda b, *_: (0, b)),
        ],
        scratch_shapes=[
            pltpu.VMEM((8, TMB), f32),
            pltpu.VMEM((8, TMB), f32),
            pltpu.VMEM((QW, TMB), f32),
        ],
    )
    pairs = count * TMB * TMB * GROUPS
    return pl.pallas_call(
        functools.partial(forward_kernel, layout),
        grid_spec=grid_spec,
        out_shape=[
            jax.ShapeDtypeStruct((QW, 2 * TMB), f32),
            jax.ShapeDtypeStruct((8, 2 * TMB), f32),
        ],
        cost_estimate=pl.CostEstimate(
            flops=pairs * 16 * HEAD_DIM,
            transcendentals=pairs,
            bytes_accessed=count * TMB * 4 * HEAD_DIM,
        ),
        compiler_params=pltpu.CompilerParams(dimension_semantics=("arbitrary",)),
        name="attention_forward",
    )(starts, ids, prefix, q_cols, kv)


def backward_kernel(
    layout, starts, ids, prefix, q_ref, kv_ref, do_ref, lse_ref, delta_ref, dq_ref, dkv_ref, acc
):
    b = pl.program_id(0)

    @pl.when(b == 0)
    def _():
        acc[...] = jnp.zeros_like(acc)

    dq_ref[...] = jnp.zeros_like(dq_ref)

    def process(j, ok):
        k_cols = kv_ref[j, :HEAD_DIM, :]
        k_rows = k_cols.T
        v_rows = kv_ref[j, HEAD_DIM:, :].T
        dk = dv = None

        def products(h):
            hs = slice(h * HEAD_DIM, (h + 1) * HEAD_DIM)
            s = mm(k_rows, q_ref[hs, :])
            if ok is not None:
                s = jnp.where(ok, s, masked_score)
            return s, mm(v_rows, do_ref[hs, :])

        ahead = [products(h) for h in range(BACKWARD_AHEAD)]
        for h in range(GROUPS):
            if h + BACKWARD_AHEAD < GROUPS:
                ahead.append(products(h + BACKWARD_AHEAD))
            s, dp = ahead.pop(0)
            hs = slice(h * HEAD_DIM, (h + 1) * HEAD_DIM)
            p = jnp.exp(s - lse_ref[h : h + 1, :])
            ds = (p * (dp - delta_ref[h : h + 1, :])).astype(bf16)
            dq_ref[hs, :] += mm(k_cols, ds)
            dk_part = mm(q_ref[hs, :], ds, NT)
            dv_part = mm(do_ref[hs, :], p.astype(bf16), NT)
            dk = dk_part if dk is None else dk + dk_part
            dv = dv_part if dv is None else dv + dv_part
        slot = layout.slot(ids, j)
        acc[slot, :HEAD_DIM, :] += dk
        acc[slot, HEAD_DIM:, :] += dv

    each_block(layout, starts, ids, prefix, process)

    @pl.when(b == 1)
    def _():
        dkv_ref[...] = acc[...].astype(bf16)


def attention_backward(layout, starts, ids, prefix, q_cols, kv, do_cols, lse, delta):
    count = kv.shape[0]
    grid_spec = pltpu.PrefetchScalarGridSpec(
        num_scalar_prefetch=3,
        grid=(2,),
        in_specs=[
            pl.BlockSpec((QW, TMB), lambda b, *_: (0, b)),
            pl.BlockSpec((count, 2 * HEAD_DIM, TMB), lambda b, *_: (0, 0, 0)),
            pl.BlockSpec((QW, TMB), lambda b, *_: (0, b)),
            pl.BlockSpec((8, TMB), lambda b, *_: (0, b)),
            pl.BlockSpec((8, TMB), lambda b, *_: (0, b)),
        ],
        out_specs=[
            pl.BlockSpec((QW, TMB), lambda b, *_: (0, b)),
            pl.BlockSpec((count, 2 * HEAD_DIM, TMB), lambda b, *_: (0, 0, 0)),
        ],
        scratch_shapes=[pltpu.VMEM((count, 2 * HEAD_DIM, TMB), f32)],
    )
    pairs = count * TMB * TMB * GROUPS
    return pl.pallas_call(
        functools.partial(backward_kernel, layout),
        grid_spec=grid_spec,
        out_shape=[
            jax.ShapeDtypeStruct((QW, 2 * TMB), f32),
            jax.ShapeDtypeStruct((count, 2 * HEAD_DIM, TMB), bf16),
        ],
        cost_estimate=pl.CostEstimate(
            flops=pairs * 24 * HEAD_DIM,
            transcendentals=pairs,
            bytes_accessed=count * TMB * 12 * HEAD_DIM,
        ),
        compiler_params=pltpu.CompilerParams(dimension_semantics=("arbitrary",)),
        name="attention_backward",
    )(starts, ids, prefix, q_cols, kv, do_cols, lse, delta)


def rotate(values, cosine, sine):
    half = HEAD_DIM // 2
    low, high = values[:, :half], values[:, half:]
    return jnp.concatenate([low * cosine - high * sine, high * cosine + low * sine], axis=1)


def unrotate(grads, cosine, sine):
    half = HEAD_DIM // 2
    low, high = grads[:, :half], grads[:, half:]
    return jnp.concatenate([low * cosine + high * sine, high * cosine - low * sine], axis=1)


def ordered(first, own, other, axis):
    return jnp.where(
        first, jnp.concatenate([own, other], axis), jnp.concatenate([other, own], axis)
    )


def on_device(
    tokens,
    cotangent,
    place,
    prefix,
    attn_norm,
    q_weight,
    q_bias,
    k_weight,
    k_bias,
    v_weight,
    v_bias,
    o_weight,
    mlp_norm,
    gate_weight,
    up_projection_weight,
    down_weight,
):
    chips = lax.axis_size("chip")
    chip = lax.axis_index("chip")
    core = lax.axis_index("core")
    rep = lax.axis_index("rep")
    lead_core = core == 0
    lead_rep = rep == 0
    direct = chips <= DIRECT_MAX
    width = q_weight.shape[1]
    rows = q_weight.shape[0]
    seq_length = min(SEQ_MAX, TMB * chips * 2)
    block_count = 2 * chips

    hop = [[(i, (i + k) % chips) for i in range(chips)] for k in range(chips)]

    def gather_chips(a):
        if not direct:
            return list(lax.all_gather(a, "chip", axis=0, tiled=False))
        return [a] + [lax.ppermute(a, "chip", hop[k]) for k in range(1, chips)]

    def scatter_chips(stacked):
        if not direct:
            return lax.psum_scatter(stacked, "chip", scatter_dimension=0, tiled=False).astype(f32)
        pieces = lax.all_to_all(stacked, "chip", split_axis=0, concat_axis=0, tiled=True)
        return jnp.sum(pieces.astype(f32), axis=0)

    cols = QW + 2 * HEAD_DIM
    with jax.named_scope("weights_qkv"):
        vectors = (attn_norm, mlp_norm, q_bias, k_bias, v_bias)
        row_pad = -(rows + len(vectors)) % 16
        vectors = [jnp.pad(v, (0, cols - v.shape[0]))[None] for v in vectors]

        def head_columns(c):
            part = jnp.concatenate(
                [
                    q_weight[:, c * QW : (c + 1) * QW],
                    k_weight[:, c * HEAD_DIM : (c + 1) * HEAD_DIM],
                    v_weight[:, c * HEAD_DIM : (c + 1) * HEAD_DIM],
                ],
                axis=1,
            )
            return jnp.concatenate([part, *vectors, jnp.zeros((row_pad, cols), bf16)], axis=0)

        columns = (head_columns(0), head_columns(1))
        own_columns = jnp.where(lead_core, columns[0], columns[1])
        sent_columns = jnp.where(lead_core, columns[1], columns[0])
        chip_rows = ordered(lead_core, own_columns[None], swap(sent_columns, "core")[None], 0)
        qkv_all = lax.all_gather(chip_rows, "chip", axis=0, tiled=False)
        qkv_full = qkv_all[:, :, :rows].reshape(width, cols)
        vec_all = qkv_all[:, :, rows : rows + len(vectors)].astype(f32)
        vec_all = vec_all.reshape(2 * chips, len(vectors), cols)
        kv_rows = k_bias.shape[0]
        gain_one = vec_all[:, 0, :rows].reshape(1, width)
        gain_two = vec_all[:, 1, :rows].reshape(1, width)
        q_add = vec_all[:, 2, :rows].reshape(2, QW)
        k_add = vec_all[:, 3, :kv_rows].reshape(2, HEAD_DIM)
        v_add = vec_all[:, 4, :kv_rows].reshape(2, HEAD_DIM)
        biases = jnp.concatenate([q_add, k_add, v_add], axis=1)
        bias_col = jnp.where(lead_core, biases[0], biases[1])[:, None]

    with jax.named_scope("weights_mlp"):
        after = chip_rows[1, 0, 0] * 0
        gate_weight, up_projection_weight = gate_weight + after, up_projection_weight + after
        ff_rows = down_weight.shape[0]
        half_rows = ff_rows // 2
        half_pad = -(-half_rows // 16) * 16
        quarter = chips * half_pad

        down_half = jnp.where(lead_rep, down_weight[:half_rows], down_weight[half_rows:])
        o_pair = ordered(lead_core, o_weight, swap(o_weight, "core"), 0)
        down_half = jnp.pad(down_half, ((0, half_pad - half_rows), (0, 0)))

        def quarter_columns(w, c):
            split = w.reshape(rows, chips, 2, 2, half_rows)[:, :, c]
            part = jnp.where(lead_rep, split[:, :, 0], split[:, :, 1])
            return jnp.pad(part, ((0, 0), (0, 0), (0, half_pad - half_rows))).reshape(rows, quarter)

        def quarter_pair(c):
            return jnp.concatenate(
                [quarter_columns(gate_weight, c), quarter_columns(up_projection_weight, c)], axis=1
            )

        pairs = (quarter_pair(0), quarter_pair(1))
        own_pair = jnp.where(lead_core, pairs[0], pairs[1])
        sent_pair = jnp.where(lead_core, pairs[1], pairs[0])
        pair_rows = ordered(lead_core, own_pair, swap(sent_pair, "core"), 0)

    with jax.named_scope("visibility"):
        starts = place.reshape(-1, TMB)[:, 0]
        ids = jnp.stack([rep, chip, core]).astype(jnp.int32)
        layouts = [Layout(m, chips, seq_length, direct) for m in range(MB)]

    own_rows = MB * TMB

    def group_rows(a):
        both = jnp.concatenate([a, swap(a, "rep")], axis=0)
        return jnp.concatenate([both, swap(both, "core")], axis=0)

    def core_pair_sum(a):
        half = a.shape[0] // 2
        return a[:half].astype(f32) + swap(a[half:].astype(bf16), "core").astype(f32)

    def rep_pair_sum(a):
        half = a.shape[0] // 2
        return a[:half] + swap(a[half:].astype(bf16), "rep").astype(f32)

    def micro(a, m):
        return jnp.concatenate(
            [a[:, m * TMB : (m + 1) * TMB], a[:, own_rows + m * TMB : own_rows + (m + 1) * TMB]],
            axis=1,
        )

    def both_micros(parts):
        return jnp.concatenate([p[:, :TMB] for p in parts] + [p[:, TMB:] for p in parts], axis=1)

    with jax.named_scope("gather_cotangent"):
        cot_rep = swap(cotangent, "rep")
        cot_parts = (cotangent, cot_rep, swap(cotangent, "core"), swap(cot_rep, "core"))
        qkv_full, cot_parts = lax.optimization_barrier((qkv_full, cot_parts))
        cot_group = jnp.concatenate(cot_parts, axis=0)
    with jax.named_scope("project"):
        x = tokens.astype(f32)
        pair = jnp.concatenate([tokens, swap(tokens, "core")], axis=0).astype(f32)
        r_pair = lax.rsqrt(jnp.mean(pair * pair, axis=-1, keepdims=True) + norm_eps)
        normed = (pair * r_pair * gain_one).astype(bf16)
        qkv = mm(qkv_full, normed, ((0,), (1,))) + bias_col
        exponent = jnp.arange(HEAD_DIM // 2).astype(f32) * (2.0 / HEAD_DIM)
        frequency = (rope_base ** (-exponent))[:, None]
        pos = lax.dynamic_slice_in_dim(starts, (rep * chips + chip) * 2 * MB, 2 * MB) % seq_length
        pos = ordered(lead_core, pos[:MB], pos[MB:], 0)
        pos = (pos[:, None] + jnp.arange(TMB)[None]).reshape(1, 2 * own_rows)
        angles = frequency * pos.astype(f32)
        cosine, sine = jnp.cos(angles)[None], jnp.sin(angles)[None]
        k_rot = rotate(qkv[None, QW : QW + HEAD_DIM], cosine, sine)[0].astype(bf16)
        kv_own = jnp.concatenate([k_rot, qkv[QW + HEAD_DIM :].astype(bf16)], axis=0)
        q_rot = rotate(qkv[:QW].reshape(GROUPS, HEAD_DIM, 2 * own_rows), cosine, sine)
        q_all = (q_rot.astype(bf16) * HEAD_DIM**-0.5).astype(bf16).reshape(QW, 2 * own_rows)
        q_cols = [micro(q_all, m) for m in range(MB)]
    with jax.named_scope("gather_keys"):
        mine = [micro(kv_own, m) for m in range(MB)]
        mine = jnp.stack([a[:, b * TMB : (b + 1) * TMB] for a in mine for b in range(2)], axis=0)
        every = gather_chips(mine)
        kv = [
            jnp.concatenate([part[2 * m : 2 * m + 2] for part in every], axis=0)
            for m in range(MB)
        ]
    with jax.named_scope("gather_mlp"):
        strips = []
        for at in range(0, 2 * quarter, width):
            strip = pair_rows[:, at : at + width]
            strips.append(jnp.pad(strip, ((0, 0), (0, width - strip.shape[1]))))
        stack = jnp.concatenate([o_pair] + strips, axis=0)
        stack = jnp.pad(stack, ((0, -stack.shape[0] % 16), (0, 0)))
        down_half, stack = lax.optimization_barrier((down_half, stack))
        stack = lax.all_gather(stack, "chip", axis=0, tiled=False)
        down = lax.all_gather(down_half, "chip", axis=0, tiled=True)
        o_full = stack[:, : 2 * rows].reshape(width, width)
        gate_up = jnp.concatenate(
            [
                stack[:, 2 * rows * (i + 1) : 2 * rows * (i + 2)].reshape(width, width)
                for i in range(len(strips))
            ],
            axis=1,
        )[:, : 2 * quarter]

    heads, lse = [], []
    for m in range(MB):
        o_m, lse_m = attention_forward(layouts[m], starts, ids, prefix, q_cols[m], kv[m])
        heads.append(o_m)
        lse.append(lse_m)
    with jax.named_scope("attention_out"):
        att = both_micros([h.astype(bf16) for h in heads])
        att_cols = ordered(lead_core, att[:, :own_rows], swap(att[:, own_rows:], "core"), 0)
        middle = x + mm(att_cols, o_full, TN)
        r2 = lax.rsqrt(jnp.mean(middle * middle, axis=-1, keepdims=True) + norm_eps)
        normed_two = (middle * r2 * gain_two).astype(bf16)
        n2_group = group_rows(normed_two)
    with jax.named_scope("feed_forward"):
        gate_up_pre = mm(n2_group, gate_up)
        gate, up = gate_up_pre[:, :quarter], gate_up_pre[:, quarter:]
        sig = jax.nn.sigmoid(gate)
        silu = gate * sig
        hidden = (silu * up).astype(bf16)
    with jax.named_scope("feed_forward_grad"):
        dh = mm(cot_group, down, NT)
        dgate = (dh * up * (sig * (1.0 + gate * (1.0 - sig)))).astype(bf16)
        dup = (dh * silu).astype(bf16)
        dgu = jnp.concatenate([dgate, dup], axis=1)
        dn2_half = core_pair_sum(mm(dgu, gate_up, NT).astype(bf16))
        dn2_half, hidden_g, n2_g = lax.optimization_barrier((dn2_half, hidden, n2_group))
        dn2 = rep_pair_sum(dn2_half)
    with jax.named_scope("feed_forward_out"):
        result_part = mm(hidden, down).astype(bf16)

    with jax.named_scope("attention_out_grad"):
        gain_two_grad = jnp.sum(dn2 * (middle * r2), axis=0)
        e = dn2 * gain_two
        dmiddle = (
            cotangent.astype(f32)
            + r2 * e
            - middle * r2**3 * jnp.mean(e * middle, axis=-1, keepdims=True)
        )
        dbranch = dmiddle.astype(bf16)
        dbranch, result_part = lax.optimization_barrier((dbranch, result_part))
        datt = mm(o_full, dbranch, NT).astype(bf16)
        own_datt = jnp.where(lead_core, datt[:QW], datt[QW:])
        sent_datt = jnp.where(lead_core, datt[QW:], datt[:QW])
        datt_all = jnp.concatenate([own_datt, swap(sent_datt, "core")], axis=1)
    with jax.named_scope("o_weight_grad"):
        o_parts = mm(att_cols, dbranch).reshape(chips, 2, rows, width)
        o_own = jnp.where(lead_core, o_parts[:, 0], o_parts[:, 1])
        o_sent = jnp.where(lead_core, o_parts[:, 1], o_parts[:, 0])
        o_own = (o_own + swap(o_sent.astype(bf16), "core").astype(f32)).astype(bf16)
    with jax.named_scope("feed_forward_weight_grads"):
        down_grad = mm(hidden_g, cot_group, TN).astype(bf16).reshape(chips, half_pad, width)
        gate_up_grad = mm(n2_g, dgu, TN).astype(bf16).reshape(chips, 2 * rows, 2 * quarter)
        pieces = []
        for start in range(0, 2 * quarter, width):
            piece = gate_up_grad[:, :, start : start + width]
            pieces.append(jnp.pad(piece, ((0, 0), (0, 0), (0, width - piece.shape[2]))))
        blob_rows = half_pad + 2 * rows * len(pieces) + rows
        blob_pad = jnp.zeros((chips, -blob_rows % 16, width), bf16)
        blob = jnp.concatenate([down_grad] + pieces + [o_own, blob_pad], axis=1)
        blob = blob.reshape(-1, width)
        datt_all, blob = lax.optimization_barrier((datt_all, blob))
        blob_share = lax.psum_scatter(blob, "chip", scatter_dimension=0, tiled=True)
        down_share = blob_share[:half_pad]
        gate_up_share = jnp.concatenate(
            [
                blob_share[half_pad + 2 * rows * i : half_pad + 2 * rows * (i + 1)]
                for i in range(len(pieces))
            ],
            axis=1,
        )[:, : 2 * quarter]
        o_share = blob_share[blob_rows - rows : blob_rows]
    dq, dkv = [], []
    for m in range(MB):
        with jax.named_scope("attention_out_grad"):
            do_cols = micro(datt_all, m)
            delta = jnp.sum(
                (do_cols.astype(f32) * heads[m]).reshape(GROUPS, HEAD_DIM, 2 * TMB), axis=1
            )
            delta = jnp.pad(delta, ((0, 8 - GROUPS), (0, 0)))
        dq_m, dkv_m = attention_backward(
            layouts[m], starts, ids, prefix, q_cols[m], kv[m], do_cols, lse[m], delta
        )
        dq.append(dq_m)
        dkv.append(dkv_m.reshape(chips, 2, 2 * HEAD_DIM, TMB))
    with jax.named_scope("feed_forward_out"):
        result = (middle + rep_pair_sum(core_pair_sum(result_part))).astype(bf16)
    with jax.named_scope("return_keys"):
        dkv_sum = scatter_chips(jnp.stack(dkv, axis=1))
        dkv = [jnp.concatenate([dkv_sum[m, 0], dkv_sum[m, 1]], axis=1) for m in range(MB)]
    with jax.named_scope("unrotate"):
        dq_all = both_micros(dq).reshape(GROUPS, HEAD_DIM, 2 * own_rows) * HEAD_DIM**-0.5
        dq_low = unrotate(dq_all, cosine, sine).reshape(QW, 2 * own_rows).astype(bf16)
        dkv_all = both_micros(dkv)
        dk = unrotate(dkv_all[None, :HEAD_DIM], cosine, sine)[0]
        dkv_low = jnp.concatenate([dk, dkv_all[HEAD_DIM:]], axis=0).astype(bf16)

    with jax.named_scope("project_grad"):
        q_grad = mm(normed, dq_low, ((0,), (1,))).astype(bf16)
        dn1 = core_pair_sum(
            mm(dq_low, qkv_full[:, :QW], ((0,), (1,)))
            + mm(dkv_low, qkv_full[:, QW:], ((0,), (1,)))
        )
        kv_grad = mm(normed, dkv_low, ((0,), (1,))).astype(bf16)
        qkv_grad = jnp.concatenate([q_grad, kv_grad], axis=1)
        bias_grad = [jnp.sum(g.astype(f32), axis=1) for g in (dq_low, dkv_low)]
        r1 = r_pair[:own_rows]
        gain_one_grad = jnp.sum(dn1 * (x * r1), axis=0)
        e1 = dn1 * gain_one
        dx = dmiddle + r1 * e1 - x * r1**3 * jnp.mean(e1 * x, axis=-1, keepdims=True)
        input_grad = dx.astype(bf16)
    with jax.named_scope("shares"):
        vec_rows = [jnp.concatenate(bias_grad)[None]]
        for g in (gain_one_grad, gain_two_grad):
            for at in range(0, width, cols):
                piece = g[None, at : at + cols]
                vec_rows.append(jnp.pad(piece, ((0, 0), (0, cols - piece.shape[1]))))
        gain_rows = (len(vec_rows) - 1) // 2
        pack_rows = -(-len(vec_rows) // 16) * 16
        vec_rows.append(jnp.zeros((pack_rows - len(vec_rows), cols), f32))
        packed = jnp.concatenate(vec_rows, axis=0)
        share = scatter_chips(
            jnp.concatenate(
                [
                    jnp.broadcast_to(packed.astype(bf16)[None], (chips, pack_rows, cols)),
                    qkv_grad.reshape(chips, 2 * rows, cols),
                ],
                axis=1,
            )
        ).astype(bf16)

    def rep_sum(a):
        return a.astype(f32) + swap(a, "rep").astype(f32)

    with jax.named_scope("owners"):
        o_total = rep_sum(o_share)

        def both_cores(head, body):
            own = jnp.where(lead_core, body[:rows], body[rows:])
            sent = jnp.where(lead_core, body[rows:], body[:rows])
            own = jnp.concatenate([head, own], axis=0)
            other = swap(jnp.concatenate([head, sent], axis=0), "core")
            return rep_sum(ordered(lead_core, own[None], other[None], 0))

        both = both_cores(share[:pack_rows], share[pack_rows:])
        w_both = both[:, pack_rows:]
        k_at, v_at = QW, QW + HEAD_DIM
        q_total = jnp.concatenate([w_both[0, :, :k_at], w_both[1, :, :k_at]], axis=1)
        k_total = jnp.concatenate([w_both[0, :, k_at:v_at], w_both[1, :, k_at:v_at]], axis=1)
        v_total = jnp.concatenate([w_both[0, :, v_at:], w_both[1, :, v_at:]], axis=1)
        vec = both[:, 0]
        gains = both[0, 1:pack_rows] + both[1, 1:pack_rows]
        gains = [
            gains[at : at + gain_rows].reshape(gain_rows * cols)[:width] for at in (0, gain_rows)
        ]
        everything = jnp.concatenate(
            [
                vec[:, :QW].reshape(2 * QW),
                vec[:, k_at:v_at].reshape(2 * HEAD_DIM),
                vec[:, v_at:cols].reshape(2 * HEAD_DIM),
                *gains,
            ]
        )
        shard = 2 * chip + core
        vec_outs, offset = [], 0
        for size in (2 * QW, 2 * HEAD_DIM, 2 * HEAD_DIM, width, width):
            each = size // (2 * chips)
            vec_outs.append(lax.dynamic_slice_in_dim(everything, offset + shard * each, each, 0))
            offset += size
        q_b, k_b, v_b, gain_one_out, gain_two_out = vec_outs

        mine = jnp.where(lead_core, gate_up_share[:rows], gate_up_share[rows:])
        sent = jnp.where(lead_core, gate_up_share[rows:], gate_up_share[:rows])
        two = ordered(lead_core, mine[None], swap(sent, "core")[None], 0)
        four = ordered(lead_rep, two[None], swap(two, "rep")[None], 0)

        def whole_columns(part):
            part = part.reshape(2, 2, rows, chips, half_pad)[..., :half_rows]
            return part.transpose(2, 3, 1, 0, 4).reshape(rows, 4 * chips * half_rows).astype(f32)

        gate_out = whole_columns(four[..., :quarter])
        up_out = whole_columns(four[..., quarter:])
        down_mine = down_share[:half_rows]
        down_out = ordered(lead_rep, down_mine, swap(down_mine, "rep"), 0).astype(f32)

    return (
        result,
        input_grad,
        gain_one_out,
        q_total,
        q_b,
        k_total,
        k_b,
        v_total,
        v_b,
        o_total,
        gain_two_out,
        gate_out,
        up_out,
        down_out,
    )


def solution(mesh):
    split = Mesh(mesh.devices.reshape(mesh.shape["rep"], -1, 2), ("rep", "chip", "core"))
    shard = ("chip", "core")
    token_spec = P(("rep", "chip", "core"), None)
    row_spec, vec_spec = P(shard, None), P(shard)
    in_specs = (
        token_spec,
        token_spec,
        P(),
        P(),
        vec_spec,
        row_spec,
        vec_spec,
        row_spec,
        vec_spec,
        row_spec,
        vec_spec,
        row_spec,
        vec_spec,
        row_spec,
        row_spec,
        row_spec,
    )
    out_specs = (token_spec, token_spec) + in_specs[4:]
    return jax.shard_map(
        on_device, mesh=split, in_specs=in_specs, out_specs=out_specs, check_vma=False
    )
```

```python
import functools

import jax
import jax.numpy as jnp
from jax import lax
from jax.experimental import pallas as pl
from jax.experimental.pallas import tpu as pltpu
from jax.sharding import Mesh
from jax.sharding import PartitionSpec as P

HEADS = 14
KV_HEADS = 2
HEAD_DIM = 64
GROUPS = HEADS // KV_HEADS
TMB = 256
MB = 2
SEQ_MAX = 4096
QW = GROUPS * HEAD_DIM
DIRECT_MAX = 8
FORWARD_AHEAD = 4
BACKWARD_AHEAD = 2

norm_eps = 1e-06
rope_base = 1000000.0
masked_score = -1e30

bf16 = jnp.bfloat16
f32 = jnp.float32
NN = ((1,), (0,))
NT = ((1,), (1,))
TN = ((0,), (0,))


def mm(a, b, dims=NN):
    return lax.dot_general(a, b, (dims, ((), ())), preferred_element_type=f32)


def swap(a, axis):
    return lax.ppermute(a, axis, [(0, 1), (1, 0)])


class Layout:
    def __init__(self, m, chips, seq_length, rotated):
        self.m, self.chips, self.seq_length, self.rotated = m, chips, seq_length, rotated

    def start(self, starts, ids, chip, second):
        core = jnp.where(second, 1 - ids[2], ids[2])
        return starts[((ids[0] * self.chips + chip) * 2 + core) * MB + self.m]

    def query(self, starts, ids, prefix, b):
        at = self.start(starts, ids, ids[1], b == 1)
        seq = at // self.seq_length
        return seq, at - seq * self.seq_length, prefix[seq]

    def key_chip(self, ids, j):
        chip = j // 2
        if self.rotated:
            chip = ids[1] - chip
            chip = jnp.where(chip < 0, chip + self.chips, chip)
        return chip

    def slot(self, ids, j):
        return 2 * self.key_chip(ids, j) + j % 2

    def key(self, starts, ids, j):
        chip = self.key_chip(ids, j)
        at = self.start(starts, ids, chip, j % 2 == 1)
        seq = at // self.seq_length
        return seq, at - seq * self.seq_length


def each_block(layout, starts, ids, prefix, process):
    q_seq, q_pos, limit = layout.query(starts, ids, prefix, pl.program_id(0))

    def step(j, carry):
        k_seq, k_pos = layout.key(starts, ids, j)
        same = k_seq == q_seq
        full = same & ((k_pos + TMB - 1 <= q_pos) | (k_pos + TMB <= limit))
        some = same & ((k_pos <= q_pos + TMB - 1) | (k_pos < limit))

        @pl.when(full)
        def _():
            process(j, None)

        @pl.when(some & jnp.logical_not(full))
        def _():
            ks = k_pos + lax.broadcasted_iota(jnp.int32, (TMB, TMB), 0)
            qs = q_pos + lax.broadcasted_iota(jnp.int32, (TMB, TMB), 1)
            process(j, (ks <= qs) | (ks < limit))

        return carry

    lax.fori_loop(0, 2 * layout.chips, step, 0)


def forward_kernel(layout, starts, ids, prefix, q_ref, kv_ref, o_ref, lse_ref, m_s, l_s, acc):
    m_s[...] = jnp.full_like(m_s, masked_score)
    l_s[...] = jnp.zeros_like(l_s)
    acc[...] = jnp.zeros_like(acc)

    def process(j, ok):
        k_rows = kv_ref[j, :HEAD_DIM, :].T
        v_cols = kv_ref[j, HEAD_DIM:, :]
        old_max, old_sum = m_s[...], l_s[...]
        maxes, sums = [], []

        def score(h):
            s = mm(k_rows, q_ref[h * HEAD_DIM : (h + 1) * HEAD_DIM, :])
            return s if ok is None else jnp.where(ok, s, masked_score)

        ahead = [score(h) for h in range(FORWARD_AHEAD)]
        for h in range(GROUPS):
            if h + FORWARD_AHEAD < GROUPS:
                ahead.append(score(h + FORWARD_AHEAD))
            s = ahead.pop(0)
            hs = slice(h * HEAD_DIM, (h + 1) * HEAD_DIM)
            head_max = old_max[h : h + 1, :]
            new_max = jnp.maximum(head_max, jnp.max(s, axis=0, keepdims=True))
            p = jnp.exp(s - new_max)
            fade = jnp.exp(head_max - new_max)
            maxes.append(new_max)
            sums.append(old_sum[h : h + 1, :] * fade + jnp.sum(p, axis=0, keepdims=True))
            acc[hs, :] = acc[hs, :] * fade + mm(v_cols, p.astype(bf16))
        m_s[...] = jnp.concatenate(maxes + [old_max[GROUPS:]], axis=0)
        l_s[...] = jnp.concatenate(sums + [old_sum[GROUPS:]], axis=0)

    each_block(layout, starts, ids, prefix, process)
    for h in range(GROUPS):
        hs = slice(h * HEAD_DIM, (h + 1) * HEAD_DIM)
        o_ref[hs, :] = acc[hs, :] / l_s[h : h + 1, :]
    lse_ref[...] = m_s[...] + jnp.log(l_s[...])


def attention_forward(layout, starts, ids, prefix, q_cols, kv):
    count = kv.shape[0]
    grid_spec = pltpu.PrefetchScalarGridSpec(
        num_scalar_prefetch=3,
        grid=(2,),
        in_specs=[
            pl.BlockSpec((QW, TMB), lambda b, *_: (0, b)),
            pl.BlockSpec((count, 2 * HEAD_DIM, TMB), lambda b, *_: (0, 0, 0)),
        ],
        out_specs=[
            pl.BlockSpec((QW, TMB), lambda b, *_: (0, b)),
            pl.BlockSpec((8, TMB), lambda b, *_: (0, b)),
        ],
        scratch_shapes=[
            pltpu.VMEM((8, TMB), f32),
            pltpu.VMEM((8, TMB), f32),
            pltpu.VMEM((QW, TMB), f32),
        ],
    )
    pairs = count * TMB * TMB * GROUPS
    return pl.pallas_call(
        functools.partial(forward_kernel, layout),
        grid_spec=grid_spec,
        out_shape=[
            jax.ShapeDtypeStruct((QW, 2 * TMB), f32),
            jax.ShapeDtypeStruct((8, 2 * TMB), f32),
        ],
        cost_estimate=pl.CostEstimate(
            flops=pairs * 16 * HEAD_DIM,
            transcendentals=pairs,
            bytes_accessed=count * TMB * 4 * HEAD_DIM,
        ),
        compiler_params=pltpu.CompilerParams(dimension_semantics=("arbitrary",)),
        name="attention_forward",
    )(starts, ids, prefix, q_cols, kv)


def backward_kernel(
    layout, starts, ids, prefix, q_ref, kv_ref, do_ref, lse_ref, delta_ref, dq_ref, dkv_ref, acc
):
    b = pl.program_id(0)

    @pl.when(b == 0)
    def _():
        acc[...] = jnp.zeros_like(acc)

    dq_ref[...] = jnp.zeros_like(dq_ref)

    def process(j, ok):
        k_cols = kv_ref[j, :HEAD_DIM, :]
        k_rows = k_cols.T
        v_rows = kv_ref[j, HEAD_DIM:, :].T
        dk = dv = None

        def products(h):
            hs = slice(h * HEAD_DIM, (h + 1) * HEAD_DIM)
            s = mm(k_rows, q_ref[hs, :])
            if ok is not None:
                s = jnp.where(ok, s, masked_score)
            return s, mm(v_rows, do_ref[hs, :])

        ahead = [products(h) for h in range(BACKWARD_AHEAD)]
        for h in range(GROUPS):
            if h + BACKWARD_AHEAD < GROUPS:
                ahead.append(products(h + BACKWARD_AHEAD))
            s, dp = ahead.pop(0)
            hs = slice(h * HEAD_DIM, (h + 1) * HEAD_DIM)
            p = jnp.exp(s - lse_ref[h : h + 1, :])
            ds = (p * (dp - delta_ref[h : h + 1, :])).astype(bf16)
            dq_ref[hs, :] += mm(k_cols, ds)
            dk_part = mm(q_ref[hs, :], ds, NT)
            dv_part = mm(do_ref[hs, :], p.astype(bf16), NT)
            dk = dk_part if dk is None else dk + dk_part
            dv = dv_part if dv is None else dv + dv_part
        slot = layout.slot(ids, j)
        acc[slot, :HEAD_DIM, :] += dk
        acc[slot, HEAD_DIM:, :] += dv

    each_block(layout, starts, ids, prefix, process)

    @pl.when(b == 1)
    def _():
        dkv_ref[...] = acc[...].astype(bf16)


def attention_backward(layout, starts, ids, prefix, q_cols, kv, do_cols, lse, delta):
    count = kv.shape[0]
    grid_spec = pltpu.PrefetchScalarGridSpec(
        num_scalar_prefetch=3,
        grid=(2,),
        in_specs=[
            pl.BlockSpec((QW, TMB), lambda b, *_: (0, b)),
            pl.BlockSpec((count, 2 * HEAD_DIM, TMB), lambda b, *_: (0, 0, 0)),
            pl.BlockSpec((QW, TMB), lambda b, *_: (0, b)),
            pl.BlockSpec((8, TMB), lambda b, *_: (0, b)),
            pl.BlockSpec((8, TMB), lambda b, *_: (0, b)),
        ],
        out_specs=[
            pl.BlockSpec((QW, TMB), lambda b, *_: (0, b)),
            pl.BlockSpec((count, 2 * HEAD_DIM, TMB), lambda b, *_: (0, 0, 0)),
        ],
        scratch_shapes=[pltpu.VMEM((count, 2 * HEAD_DIM, TMB), f32)],
    )
    pairs = count * TMB * TMB * GROUPS
    return pl.pallas_call(
        functools.partial(backward_kernel, layout),
        grid_spec=grid_spec,
        out_shape=[
            jax.ShapeDtypeStruct((QW, 2 * TMB), f32),
            jax.ShapeDtypeStruct((count, 2 * HEAD_DIM, TMB), bf16),
        ],
        cost_estimate=pl.CostEstimate(
            flops=pairs * 24 * HEAD_DIM,
            transcendentals=pairs,
            bytes_accessed=count * TMB * 12 * HEAD_DIM,
        ),
        compiler_params=pltpu.CompilerParams(dimension_semantics=("arbitrary",)),
        name="attention_backward",
    )(starts, ids, prefix, q_cols, kv, do_cols, lse, delta)


def rotate(values, cosine, sine):
    half = HEAD_DIM // 2
    low, high = values[:, :half], values[:, half:]
    return jnp.concatenate([low * cosine - high * sine, high * cosine + low * sine], axis=1)


def unrotate(grads, cosine, sine):
    half = HEAD_DIM // 2
    low, high = grads[:, :half], grads[:, half:]
    return jnp.concatenate([low * cosine + high * sine, high * cosine - low * sine], axis=1)


def ordered(first, own, other, axis):
    return jnp.where(
        first, jnp.concatenate([own, other], axis), jnp.concatenate([other, own], axis)
    )


def on_device(
    tokens,
    cotangent,
    place,
    prefix,
    attn_norm,
    q_weight,
    q_bias,
    k_weight,
    k_bias,
    v_weight,
    v_bias,
    o_weight,
    mlp_norm,
    gate_weight,
    up_projection_weight,
    down_weight,
):
    chips = lax.axis_size("chip")
    chip = lax.axis_index("chip")
    core = lax.axis_index("core")
    rep = lax.axis_index("rep")
    lead_core = core == 0
    lead_rep = rep == 0
    direct = chips <= DIRECT_MAX
    width = q_weight.shape[1]
    rows = q_weight.shape[0]
    seq_length = min(SEQ_MAX, TMB * chips * 2)
    block_count = 2 * chips

    hop = [[(i, (i + k) % chips) for i in range(chips)] for k in range(chips)]

    def gather_chips(a):
        if not direct:
            return list(lax.all_gather(a, "chip", axis=0, tiled=False))
        return [a] + [lax.ppermute(a, "chip", hop[k]) for k in range(1, chips)]

    def scatter_chips(stacked):
        if not direct:
            return lax.psum_scatter(stacked, "chip", scatter_dimension=0, tiled=False).astype(f32)
        pieces = lax.all_to_all(stacked, "chip", split_axis=0, concat_axis=0, tiled=True)
        return jnp.sum(pieces.astype(f32), axis=0)

    cols = QW + 2 * HEAD_DIM
    with jax.named_scope("weights_qkv"):
        vectors = (attn_norm, mlp_norm, q_bias, k_bias, v_bias)
        row_pad = -(rows + len(vectors)) % 16
        vectors = [jnp.pad(v, (0, cols - v.shape[0]))[None] for v in vectors]

        def head_columns(c):
            part = jnp.concatenate(
                [
                    q_weight[:, c * QW : (c + 1) * QW],
                    k_weight[:, c * HEAD_DIM : (c + 1) * HEAD_DIM],
                    v_weight[:, c * HEAD_DIM : (c + 1) * HEAD_DIM],
                ],
                axis=1,
            )
            return jnp.concatenate([part, *vectors, jnp.zeros((row_pad, cols), bf16)], axis=0)

        columns = (head_columns(0), head_columns(1))
        own_columns = jnp.where(lead_core, columns[0], columns[1])
        sent_columns = jnp.where(lead_core, columns[1], columns[0])
        chip_rows = ordered(lead_core, own_columns[None], swap(sent_columns, "core")[None], 0)
        qkv_all = lax.all_gather(chip_rows, "chip", axis=0, tiled=False)
        qkv_full = qkv_all[:, :, :rows].reshape(width, cols)
        vec_all = qkv_all[:, :, rows : rows + len(vectors)].astype(f32)
        vec_all = vec_all.reshape(2 * chips, len(vectors), cols)
        kv_rows = k_bias.shape[0]
        gain_one = vec_all[:, 0, :rows].reshape(1, width)
        gain_two = vec_all[:, 1, :rows].reshape(1, width)
        q_add = vec_all[:, 2, :rows].reshape(2, QW)
        k_add = vec_all[:, 3, :kv_rows].reshape(2, HEAD_DIM)
        v_add = vec_all[:, 4, :kv_rows].reshape(2, HEAD_DIM)
        biases = jnp.concatenate([q_add, k_add, v_add], axis=1)
        bias_col = jnp.where(lead_core, biases[0], biases[1])[:, None]

    with jax.named_scope("weights_mlp"):
        after = chip_rows[1, 0, 0] * 0
        gate_weight, up_projection_weight = gate_weight + after, up_projection_weight + after
        ff_rows = down_weight.shape[0]
        half_rows = ff_rows // 2
        half_pad = -(-half_rows // 16) * 16
        quarter = chips * half_pad

        down_half = jnp.where(lead_rep, down_weight[:half_rows], down_weight[half_rows:])
        o_pair = ordered(lead_core, o_weight, swap(o_weight, "core"), 0)
        down_half = jnp.pad(down_half, ((0, half_pad - half_rows), (0, 0)))

        def quarter_columns(w, c):
            split = w.reshape(rows, chips, 2, 2, half_rows)[:, :, c]
            part = jnp.where(lead_rep, split[:, :, 0], split[:, :, 1])
            return jnp.pad(part, ((0, 0), (0, 0), (0, half_pad - half_rows))).reshape(rows, quarter)

        def quarter_pair(c):
            return jnp.concatenate(
                [quarter_columns(gate_weight, c), quarter_columns(up_projection_weight, c)], axis=1
            )

        pairs = (quarter_pair(0), quarter_pair(1))
        own_pair = jnp.where(lead_core, pairs[0], pairs[1])
        sent_pair = jnp.where(lead_core, pairs[1], pairs[0])
        pair_rows = ordered(lead_core, own_pair, swap(sent_pair, "core"), 0)

    with jax.named_scope("visibility"):
        starts = place.reshape(-1, TMB)[:, 0]
        ids = jnp.stack([rep, chip, core]).astype(jnp.int32)
        layouts = [Layout(m, chips, seq_length, direct) for m in range(MB)]

    own_rows = MB * TMB

    def group_rows(a):
        both = jnp.concatenate([a, swap(a, "rep")], axis=0)
        return jnp.concatenate([both, swap(both, "core")], axis=0)

    def core_pair_sum(a):
        half = a.shape[0] // 2
        return a[:half].astype(f32) + swap(a[half:].astype(bf16), "core").astype(f32)

    def rep_pair_sum(a):
        half = a.shape[0] // 2
        return a[:half] + swap(a[half:].astype(bf16), "rep").astype(f32)

    def micro(a, m):
        return jnp.concatenate(
            [a[:, m * TMB : (m + 1) * TMB], a[:, own_rows + m * TMB : own_rows + (m + 1) * TMB]],
            axis=1,
        )

    def both_micros(parts):
        return jnp.concatenate([p[:, :TMB] for p in parts] + [p[:, TMB:] for p in parts], axis=1)

    with jax.named_scope("gather_cotangent"):
        cot_rep = swap(cotangent, "rep")
        cot_parts = (cotangent, cot_rep, swap(cotangent, "core"), swap(cot_rep, "core"))
        qkv_full, cot_parts = lax.optimization_barrier((qkv_full, cot_parts))
        cot_group = jnp.concatenate(cot_parts, axis=0)
    with jax.named_scope("project"):
        x = tokens.astype(f32)
        pair = jnp.concatenate([tokens, swap(tokens, "core")], axis=0).astype(f32)
        r_pair = lax.rsqrt(jnp.mean(pair * pair, axis=-1, keepdims=True) + norm_eps)
        normed = (pair * r_pair * gain_one).astype(bf16)
        qkv = mm(qkv_full, normed, ((0,), (1,))) + bias_col
        exponent = jnp.arange(HEAD_DIM // 2).astype(f32) * (2.0 / HEAD_DIM)
        frequency = (rope_base ** (-exponent))[:, None]
        pos = lax.dynamic_slice_in_dim(starts, (rep * chips + chip) * 2 * MB, 2 * MB) % seq_length
        pos = ordered(lead_core, pos[:MB], pos[MB:], 0)
        pos = (pos[:, None] + jnp.arange(TMB)[None]).reshape(1, 2 * own_rows)
        angles = frequency * pos.astype(f32)
        cosine, sine = jnp.cos(angles)[None], jnp.sin(angles)[None]
        k_rot = rotate(qkv[None, QW : QW + HEAD_DIM], cosine, sine)[0].astype(bf16)
        kv_own = jnp.concatenate([k_rot, qkv[QW + HEAD_DIM :].astype(bf16)], axis=0)
        q_rot = rotate(qkv[:QW].reshape(GROUPS, HEAD_DIM, 2 * own_rows), cosine, sine)
        q_all = (q_rot.astype(bf16) * HEAD_DIM**-0.5).astype(bf16).reshape(QW, 2 * own_rows)
        q_cols = [micro(q_all, m) for m in range(MB)]
    with jax.named_scope("gather_keys"):
        mine = [micro(kv_own, m) for m in range(MB)]
        mine = jnp.stack([a[:, b * TMB : (b + 1) * TMB] for a in mine for b in range(2)], axis=0)
        every = gather_chips(mine)
        kv = [
            jnp.concatenate([part[2 * m : 2 * m + 2] for part in every], axis=0)
            for m in range(MB)
        ]
    with jax.named_scope("gather_mlp"):
        strips = []
        for at in range(0, 2 * quarter, width):
            strip = pair_rows[:, at : at + width]
            strips.append(jnp.pad(strip, ((0, 0), (0, width - strip.shape[1]))))
        stack = jnp.concatenate([o_pair] + strips, axis=0)
        stack = jnp.pad(stack, ((0, -stack.shape[0] % 16), (0, 0)))
        down_half, stack = lax.optimization_barrier((down_half, stack))
        stack = lax.all_gather(stack, "chip", axis=0, tiled=False)
        down = lax.all_gather(down_half, "chip", axis=0, tiled=True)
        o_full = stack[:, : 2 * rows].reshape(width, width)
        gate_up = jnp.concatenate(
            [
                stack[:, 2 * rows * (i + 1) : 2 * rows * (i + 2)].reshape(width, width)
                for i in range(len(strips))
            ],
            axis=1,
        )[:, : 2 * quarter]

    heads, lse = [], []
    for m in range(MB):
        o_m, lse_m = attention_forward(layouts[m], starts, ids, prefix, q_cols[m], kv[m])
        heads.append(o_m)
        lse.append(lse_m)
    with jax.named_scope("attention_out"):
        att = both_micros([h.astype(bf16) for h in heads])
        att_cols = ordered(lead_core, att[:, :own_rows], swap(att[:, own_rows:], "core"), 0)
        middle = x + mm(att_cols, o_full, TN)
        r2 = lax.rsqrt(jnp.mean(middle * middle, axis=-1, keepdims=True) + norm_eps)
        normed_two = (middle * r2 * gain_two).astype(bf16)
        n2_group = group_rows(normed_two)
    with jax.named_scope("feed_forward"):
        gate_up_pre = mm(n2_group, gate_up)
        gate, up = gate_up_pre[:, :quarter], gate_up_pre[:, quarter:]
        sig = jax.nn.sigmoid(gate)
        silu = gate * sig
        hidden = (silu * up).astype(bf16)
    with jax.named_scope("feed_forward_grad"):
        dh = mm(cot_group, down, NT)
        dgate = (dh * up * (sig * (1.0 + gate * (1.0 - sig)))).astype(bf16)
        dup = (dh * silu).astype(bf16)
        dgu = jnp.concatenate([dgate, dup], axis=1)
        dn2_half = core_pair_sum(mm(dgu, gate_up, NT).astype(bf16))
        dn2_half, hidden_g, n2_g = lax.optimization_barrier((dn2_half, hidden, n2_group))
        dn2 = rep_pair_sum(dn2_half)
    with jax.named_scope("feed_forward_out"):
        result_part = mm(hidden, down).astype(bf16)

    with jax.named_scope("attention_out_grad"):
        gain_two_grad = jnp.sum(dn2 * (middle * r2), axis=0)
        e = dn2 * gain_two
        dmiddle = (
            cotangent.astype(f32)
            + r2 * e
            - middle * r2**3 * jnp.mean(e * middle, axis=-1, keepdims=True)
        )
        dbranch = dmiddle.astype(bf16)
        dbranch, result_part = lax.optimization_barrier((dbranch, result_part))
        datt = mm(o_full, dbranch, NT).astype(bf16)
        own_datt = jnp.where(lead_core, datt[:QW], datt[QW:])
        sent_datt = jnp.where(lead_core, datt[QW:], datt[:QW])
        datt_all = jnp.concatenate([own_datt, swap(sent_datt, "core")], axis=1)
    with jax.named_scope("o_weight_grad"):
        o_parts = mm(att_cols, dbranch).reshape(chips, 2, rows, width)
        o_own = jnp.where(lead_core, o_parts[:, 0], o_parts[:, 1])
        o_sent = jnp.where(lead_core, o_parts[:, 1], o_parts[:, 0])
        o_own = (o_own + swap(o_sent.astype(bf16), "core").astype(f32)).astype(bf16)
    with jax.named_scope("feed_forward_weight_grads"):
        down_grad = mm(hidden_g, cot_group, TN).astype(bf16).reshape(chips, half_pad, width)
        gate_up_grad = mm(n2_g, dgu, TN).astype(bf16).reshape(chips, 2 * rows, 2 * quarter)
        pieces = []
        for start in range(0, 2 * quarter, width):
            piece = gate_up_grad[:, :, start : start + width]
            pieces.append(jnp.pad(piece, ((0, 0), (0, 0), (0, width - piece.shape[2]))))
        blob_rows = half_pad + 2 * rows * len(pieces) + rows
        blob_pad = jnp.zeros((chips, -blob_rows % 16, width), bf16)
        blob = jnp.concatenate([down_grad] + pieces + [o_own, blob_pad], axis=1)
        blob = blob.reshape(-1, width)
        datt_all, blob = lax.optimization_barrier((datt_all, blob))
        blob_share = lax.psum_scatter(blob, "chip", scatter_dimension=0, tiled=True)
        down_share = blob_share[:half_pad]
        gate_up_share = jnp.concatenate(
            [
                blob_share[half_pad + 2 * rows * i : half_pad + 2 * rows * (i + 1)]
                for i in range(len(pieces))
            ],
            axis=1,
        )[:, : 2 * quarter]
        o_share = blob_share[blob_rows - rows : blob_rows]
    dq, dkv = [], []
    for m in range(MB):
        with jax.named_scope("attention_out_grad"):
            do_cols = micro(datt_all, m)
            delta = jnp.sum(
                (do_cols.astype(f32) * heads[m]).reshape(GROUPS, HEAD_DIM, 2 * TMB), axis=1
            )
            delta = jnp.pad(delta, ((0, 8 - GROUPS), (0, 0)))
        dq_m, dkv_m = attention_backward(
            layouts[m], starts, ids, prefix, q_cols[m], kv[m], do_cols, lse[m], delta
        )
        dq.append(dq_m)
        dkv.append(dkv_m.reshape(chips, 2, 2 * HEAD_DIM, TMB))
    with jax.named_scope("feed_forward_out"):
        result = (middle + rep_pair_sum(core_pair_sum(result_part))).astype(bf16)
    with jax.named_scope("return_keys"):
        dkv = [scatter_chips(part) for part in dkv]
        dkv = [jnp.concatenate([part[0], part[1]], axis=1) for part in dkv]
    with jax.named_scope("unrotate"):
        dq_all = both_micros(dq).reshape(GROUPS, HEAD_DIM, 2 * own_rows) * HEAD_DIM**-0.5
        dq_low = unrotate(dq_all, cosine, sine).reshape(QW, 2 * own_rows).astype(bf16)
        dkv_all = both_micros(dkv)
        dk = unrotate(dkv_all[None, :HEAD_DIM], cosine, sine)[0]
        dkv_low = jnp.concatenate([dk, dkv_all[HEAD_DIM:]], axis=0).astype(bf16)

    with jax.named_scope("project_grad"):
        q_grad = mm(normed, dq_low, ((0,), (1,))).astype(bf16)
        dn1 = core_pair_sum(
            mm(dq_low, qkv_full[:, :QW], ((0,), (1,)))
            + mm(dkv_low, qkv_full[:, QW:], ((0,), (1,)))
        )
        kv_grad = mm(normed, dkv_low, ((0,), (1,))).astype(bf16)
        qkv_grad = jnp.concatenate([q_grad, kv_grad], axis=1)
        bias_grad = [jnp.sum(g.astype(f32), axis=1) for g in (dq_low, dkv_low)]
        r1 = r_pair[:own_rows]
        gain_one_grad = jnp.sum(dn1 * (x * r1), axis=0)
        e1 = dn1 * gain_one
        dx = dmiddle + r1 * e1 - x * r1**3 * jnp.mean(e1 * x, axis=-1, keepdims=True)
        input_grad = dx.astype(bf16)
    with jax.named_scope("shares"):
        vec_rows = [jnp.concatenate(bias_grad)[None]]
        for g in (gain_one_grad, gain_two_grad):
            for at in range(0, width, cols):
                piece = g[None, at : at + cols]
                vec_rows.append(jnp.pad(piece, ((0, 0), (0, cols - piece.shape[1]))))
        gain_rows = (len(vec_rows) - 1) // 2
        pack_rows = -(-len(vec_rows) // 16) * 16
        vec_rows.append(jnp.zeros((pack_rows - len(vec_rows), cols), f32))
        packed = jnp.concatenate(vec_rows, axis=0)
        share = scatter_chips(
            jnp.concatenate(
                [
                    jnp.broadcast_to(packed.astype(bf16)[None], (chips, pack_rows, cols)),
                    qkv_grad.reshape(chips, 2 * rows, cols),
                ],
                axis=1,
            )
        ).astype(bf16)

    def rep_sum(a):
        return a.astype(f32) + swap(a, "rep").astype(f32)

    with jax.named_scope("owners"):
        mine = jnp.where(lead_core, gate_up_share[:rows], gate_up_share[rows:])
        sent = jnp.where(lead_core, gate_up_share[rows:], gate_up_share[:rows])
        two = ordered(lead_core, mine[None], swap(sent, "core")[None], 0)
        four = ordered(lead_rep, two[None], swap(two, "rep")[None], 0)

        share, four = lax.optimization_barrier((share, four))
        o_total = rep_sum(o_share)

        def both_cores(head, body):
            own = jnp.where(lead_core, body[:rows], body[rows:])
            sent = jnp.where(lead_core, body[rows:], body[:rows])
            own = jnp.concatenate([head, own], axis=0)
            other = swap(jnp.concatenate([head, sent], axis=0), "core")
            return rep_sum(ordered(lead_core, own[None], other[None], 0))

        both = both_cores(share[:pack_rows], share[pack_rows:])
        w_both = both[:, pack_rows:]
        k_at, v_at = QW, QW + HEAD_DIM
        q_total = jnp.concatenate([w_both[0, :, :k_at], w_both[1, :, :k_at]], axis=1)
        k_total = jnp.concatenate([w_both[0, :, k_at:v_at], w_both[1, :, k_at:v_at]], axis=1)
        v_total = jnp.concatenate([w_both[0, :, v_at:], w_both[1, :, v_at:]], axis=1)
        vec = both[:, 0]
        gains = both[0, 1:pack_rows] + both[1, 1:pack_rows]
        gains = [
            gains[at : at + gain_rows].reshape(gain_rows * cols)[:width] for at in (0, gain_rows)
        ]
        everything = jnp.concatenate(
            [
                vec[:, :QW].reshape(2 * QW),
                vec[:, k_at:v_at].reshape(2 * HEAD_DIM),
                vec[:, v_at:cols].reshape(2 * HEAD_DIM),
                *gains,
            ]
        )
        shard = 2 * chip + core
        vec_outs, offset = [], 0
        for size in (2 * QW, 2 * HEAD_DIM, 2 * HEAD_DIM, width, width):
            each = size // (2 * chips)
            vec_outs.append(lax.dynamic_slice_in_dim(everything, offset + shard * each, each, 0))
            offset += size
        q_b, k_b, v_b, gain_one_out, gain_two_out = vec_outs

        def whole_columns(part):
            part = part.reshape(2, 2, rows, chips, half_pad)[..., :half_rows]
            return part.transpose(2, 3, 1, 0, 4).reshape(rows, 4 * chips * half_rows).astype(f32)

        gate_out = whole_columns(four[..., :quarter])
        up_out = whole_columns(four[..., quarter:])
        down_mine = down_share[:half_rows]
        down_out = ordered(lead_rep, down_mine, swap(down_mine, "rep"), 0).astype(f32)

    return (
        result,
        input_grad,
        gain_one_out,
        q_total,
        q_b,
        k_total,
        k_b,
        v_total,
        v_b,
        o_total,
        gain_two_out,
        gate_out,
        up_out,
        down_out,
    )


def solution(mesh):
    split = Mesh(mesh.devices.reshape(mesh.shape["rep"], -1, 2), ("rep", "chip", "core"))
    shard = ("chip", "core")
    token_spec = P(("rep", "chip", "core"), None)
    row_spec, vec_spec = P(shard, None), P(shard)
    in_specs = (
        token_spec,
        token_spec,
        P(),
        P(),
        vec_spec,
        row_spec,
        vec_spec,
        row_spec,
        vec_spec,
        row_spec,
        vec_spec,
        row_spec,
        vec_spec,
        row_spec,
        row_spec,
        row_spec,
    )
    out_specs = (token_spec, token_spec) + in_specs[4:]
    return jax.shard_map(
        on_device, mesh=split, in_specs=in_specs, out_specs=out_specs, check_vma=False
    )
```
